512 devices in a mesh: mem: 64 (over z, y), ctx: 8 (over x, core).
Axes of the slice: x: 4, y: 8, z: 8, core: 2. Of those that a mesh axis runs over, the one named last changes fastest.
Arguments:
- queries: bfloat16 [32768, 4096], P(('mem', 'ctx')), may hold values from -400 to 400, as said below
- local_keys: bfloat16 [32768, 1024], P(('mem', 'ctx')), may hold values from -6 to 6
- local_values: bfloat16 [32768, 1024], P(('mem', 'ctx')), may hold values from -6 to 6
- mem_keys: bfloat16 [8192, 1024], P('mem'), may hold values from -6 to 6
- mem_values: bfloat16 [8192, 1024], P('mem'), may hold values from -6 to 6
- block_ids: int32 [2048, 16], P(('mem', 'ctx')), may hold values from 0 to 255, as said below
- gate_bias: float32 [32], replicated, may hold values from -3 to 3
Outputs:
- attended: bfloat16 [32768, 4096], P(('mem', 'ctx'))
The draws below stay inside these ranges and needn't reach their ends.
Inputs may be any that keep to these rules, and one draw needn't show every extreme that they name: `block_ids`: the 16 blocks of one query block lie on 16 different indices of mem, block j lying on index j // 4; the 4 query blocks of rows q * 4 to (q + 1) * 4 - 1 together name every index of mem exactly once; some blocks are asked for far more often than others. `queries`: each query head's entries may carry a common scale.
All inputs are finite; a program needn't handle non-finite values.
Results may differ from the reference program's by a relative error of at most 0.005.
Values may be sent and summed in bfloat16 or wider, within the bound.
No kernel may reach another device: no remote copies, remote signals or barrier semaphores. Data moves between devices by JAX's collectives and lax.ppermute only.
A program may use at most 64 MiB of HBM per device.

```python
import jax
import jax.numpy as jnp
from jax import lax

HEADS = 32
KV_HEADS = 8
HEAD_DIM = 128
Q_DEV = 64
MB_DEV = 4
BLOCK = 32
TOPB = 16
QB_DEV = 4
QBLOCK = 16
SPAN = 512
QBLOCKS = 2048
TOKENS = 32768
MEM_BLOCKS = 256
MEM_TOKENS = 8192
N_MEM = 64
N_CTX = 8


def draw_queries(key, part):
    base = jnp.clip(jax.random.normal(key, (TOKENS, HEADS, HEAD_DIM), jnp.float32), -5.0, 5.0)
    return base.reshape(TOKENS, HEADS * HEAD_DIM).astype(jnp.bfloat16)


def draw_block_ids(key, part):
    first_key = jax.random.fold_in(key, 11)
    third_key = jax.random.fold_in(key, 13)
    requesters = QBLOCKS // QB_DEV
    holders = jnp.arange(N_MEM, dtype=jnp.int32)
    noise = jax.random.randint(first_key, (requesters, N_MEM), 0, 2 ** 20)
    scores = noise * N_MEM + holders[None, :]
    owners = jnp.argsort(scores, axis=1).astype(jnp.int32).reshape(QBLOCKS, TOPB)
    draws = jax.random.randint(third_key, (QBLOCKS, TOPB), 0, 2 * MB_DEV)
    slots = jnp.where(draws < MB_DEV, 0, draws - MB_DEV)
    row_zero = (jnp.arange(QBLOCKS, dtype=jnp.int32) < QB_DEV)[:, None]
    slots = jnp.where(row_zero & (owners == 0), 0, slots)
    slots = jnp.where(row_zero & (owners == N_MEM - 1), MB_DEV - 1, slots)
    return (owners * MB_DEV + slots).astype(jnp.int32)


def steps_of(own_key, extent, split, low, high):
    gain, own = 1.0, jax.random.fold_in(own_key, 6)
    for position, shards_of in split:
        steps = jnp.exp(jax.random.uniform(jax.random.fold_in(own, position), (shards_of,), jnp.float32, low / len(split), high / len(split)))
        gain = gain * jnp.repeat(steps, extent[position] // shards_of).reshape([-1 if axis == position else 1 for axis in range(len(extent))])
    return gain


def scatter_about(rng, extent, deviation, reach, shards=(), kind=jnp.bfloat16):
    level = steps_of(rng, extent, shards, -0.22, 0.18) if shards else 1.0
    values = jax.random.normal(rng, extent, jnp.float32) * deviation * level
    return jnp.minimum(jnp.maximum(values, -reach), reach).astype(kind)


def setup_inputs(seed: int = 0) -> dict:
    seeds = jax.random.split(jax.random.key(seed), 8)
    queries = draw_queries(jax.random.fold_in(seeds[7], 71), 0)
    local_keys = scatter_about(seeds[1], (TOKENS, KV_HEADS * HEAD_DIM), 1.0, 6.0, ((0, 512),))
    local_values = scatter_about(seeds[2], (TOKENS, KV_HEADS * HEAD_DIM), 1.0, 6.0, ((0, 512),))
    mem_keys = scatter_about(seeds[3], (MEM_TOKENS, KV_HEADS * HEAD_DIM), 1.0, 6.0, ((0, 64),))
    mem_values = scatter_about(seeds[4], (MEM_TOKENS, KV_HEADS * HEAD_DIM), 1.0, 6.0, ((0, 64),))
    block_ids = draw_block_ids(jax.random.fold_in(seeds[7], 71), 0)
    gate_bias = jnp.clip(jax.random.uniform(seeds[6], (HEADS,), jnp.float32, -3.0, 3.0), -3.0, 3.0)
    return {"queries": queries, "local_keys": local_keys, "local_values": local_values, "mem_keys": mem_keys, "mem_values": mem_values, "block_ids": block_ids, "gate_bias": gate_bias}


def reference(queries, local_keys, local_values, mem_keys, mem_values, block_ids, gate_bias):
    groups = HEADS // KV_HEADS
    scale = HEAD_DIM ** -0.5
    key_blocks = mem_keys.reshape(MEM_BLOCKS, BLOCK, KV_HEADS, HEAD_DIM)
    value_blocks = mem_values.reshape(MEM_BLOCKS, BLOCK, KV_HEADS, HEAD_DIM)
    gate = jax.nn.sigmoid(gate_bias.astype(jnp.float32)).reshape(KV_HEADS, groups)[None, :, :, None]

    def one_block(index):
        span = index // N_CTX
        within = index % N_CTX
        query_rows = lax.dynamic_slice_in_dim(queries, (index * Q_DEV).astype(jnp.int32), Q_DEV, 0)
        query_heads = query_rows.reshape(Q_DEV, KV_HEADS, groups, HEAD_DIM).astype(jnp.float32)
        start = (span * SPAN).astype(jnp.int32)
        span_keys = lax.dynamic_slice_in_dim(local_keys, start, SPAN, 0).reshape(SPAN, KV_HEADS, HEAD_DIM).astype(jnp.float32)
        span_values = lax.dynamic_slice_in_dim(local_values, start, SPAN, 0).reshape(SPAN, KV_HEADS, HEAD_DIM).astype(jnp.float32)
        scores = jnp.einsum("qhgd,khd->hgqk", query_heads, span_keys) * scale
        query_pos = within * Q_DEV + jnp.arange(Q_DEV, dtype=jnp.int32)
        key_pos = jnp.arange(SPAN, dtype=jnp.int32)
        allowed = (key_pos[None, :] <= query_pos[:, None])[None, None]
        scores = jnp.where(allowed, scores, -1e30)
        top = jnp.max(scores, axis=-1, keepdims=True)
        weights = jnp.where(allowed, jnp.exp(scores - top), 0.0)
        total = jnp.sum(weights, axis=-1)
        rounded = weights.astype(jnp.bfloat16).astype(jnp.float32)
        local_out = jnp.einsum("hgqk,khd->qhgd", rounded, span_values) / jnp.transpose(total, (2, 0, 1))[..., None]
        picked = lax.dynamic_slice_in_dim(block_ids, (index * QB_DEV).astype(jnp.int32), QB_DEV, 0)
        fetched_keys = key_blocks[picked].reshape(QB_DEV, TOPB * BLOCK, KV_HEADS, HEAD_DIM).astype(jnp.float32)
        fetched_values = value_blocks[picked].reshape(QB_DEV, TOPB * BLOCK, KV_HEADS, HEAD_DIM).astype(jnp.float32)
        block_heads = query_heads.reshape(QB_DEV, QBLOCK, KV_HEADS, groups, HEAD_DIM)
        mem_scores = jnp.einsum("bqhgd,bkhd->bhgqk", block_heads, fetched_keys) * scale
        mem_top = jnp.max(mem_scores, axis=-1, keepdims=True)
        mem_weights = jnp.exp(mem_scores - mem_top)
        mem_total = jnp.sum(mem_weights, axis=-1)
        mem_rounded = mem_weights.astype(jnp.bfloat16).astype(jnp.float32)
        mem_out = jnp.einsum("bhgqk,bkhd->bqhgd", mem_rounded, fetched_values) / jnp.transpose(mem_total, (0, 3, 1, 2))[..., None]
        mem_out = mem_out.reshape(Q_DEV, KV_HEADS, groups, HEAD_DIM)
        mixed = gate * mem_out + (1.0 - gate) * local_out
        return mixed.reshape(Q_DEV, HEADS * HEAD_DIM).astype(jnp.bfloat16)

    result = lax.map(one_block, jnp.arange(N_MEM * N_CTX, dtype=jnp.int32))
    return result.reshape(TOKENS, HEADS * HEAD_DIM)
```

```python
import functools

import jax
import jax.numpy as jnp
from jax import lax
from jax.experimental import pallas as pl
from jax.experimental.pallas import tpu as pltpu
from jax.sharding import PartitionSpec as P

HEADS = 32
KV_HEADS = 8
GROUPS = HEADS // KV_HEADS
HEAD_DIM = 128
BLOCK = 32
TOPB = 16
QBLOCK = 16
LANES = GROUPS * HEAD_DIM
EXP2_SCALE = HEAD_DIM ** (-0.5) * 1.4426950408889634
NEG = -1e30
TILE = 128


def product(left, right, contract_right):
    return lax.dot_general(
        left, right, (((1,), (contract_right,)), ((), ())), preferred_element_type=jnp.float32
    )


def softmax_parts(scores):
    top = jnp.max(scores, axis=-1, keepdims=True)
    weights = jnp.exp2((scores - top) * EXP2_SCALE)
    return weights, jnp.sum(weights, axis=-1, keepdims=True)


def heads_to_rows(rows):
    return jnp.concatenate(
        [rows[:, h * HEAD_DIM : (h + 1) * HEAD_DIM] for h in range(GROUPS)], axis=0
    )


def local_kernel(qkv_ref, out_ref):
    span = qkv_ref.shape[0]
    for tile in range(span // TILE):
        lo, hi = tile * TILE, (tile + 1) * TILE
        query = heads_to_rows(qkv_ref[lo:hi, :LANES])
        keys = qkv_ref[:hi, LANES : LANES + HEAD_DIM]
        values = qkv_ref[:hi, LANES + HEAD_DIM : LANES + 2 * HEAD_DIM]
        scores = product(query, keys, 1)
        row = lax.broadcasted_iota(jnp.int32, scores.shape, 0) % TILE + lo
        col = lax.broadcasted_iota(jnp.int32, scores.shape, 1)
        scores = jnp.where(col <= row, scores, NEG)
        weights, total = softmax_parts(scores)
        summed = product(weights.astype(jnp.bfloat16), values, 0) / total
        for h in range(GROUPS):
            out_ref[lo:hi, h * HEAD_DIM : (h + 1) * HEAD_DIM] = summed[
                h * TILE : (h + 1) * TILE
            ]


def memory_kernel(ids_ref, bias_ref, qkv_ref, keys_ref, values_ref, local_ref, out_ref):
    head = lax.axis_index("ctx")
    gates = [
        jax.nn.sigmoid(jnp.full((1, HEAD_DIM), bias_ref[head * GROUPS + h], jnp.float32))
        for h in range(GROUPS)
    ]
    query_blocks = qkv_ref.shape[0] // QBLOCK

    def one_block(index, carry):
        lo = pl.multiple_of(index * QBLOCK, QBLOCK)
        query = heads_to_rows(qkv_ref[pl.ds(lo, QBLOCK), :LANES])
        starts = [pl.multiple_of(ids_ref[index, j] * BLOCK, BLOCK) for j in range(TOPB)]
        keys = jnp.concatenate([keys_ref[pl.ds(s, BLOCK), :] for s in starts], axis=0)
        values = jnp.concatenate([values_ref[pl.ds(s, BLOCK), :] for s in starts], axis=0)
        weights, total = softmax_parts(product(query, keys, 1))
        summed = product(weights.astype(jnp.bfloat16), values, 0) / total
        for h in range(GROUPS):
            lanes = slice(h * HEAD_DIM, (h + 1) * HEAD_DIM)
            local_out = local_ref[pl.ds(lo, QBLOCK), lanes]
            mixed = gates[h] * summed[h * QBLOCK : (h + 1) * QBLOCK] + (1.0 - gates[h]) * local_out
            out_ref[pl.ds(lo, QBLOCK), lanes] = mixed.astype(jnp.bfloat16)
        return carry

    lax.fori_loop(0, query_blocks, one_block, 0, unroll=2)


def body(queries, local_keys, local_values, mem_keys, mem_values, block_ids, gate_bias):
    tokens = queries.shape[0]
    members = lax.axis_size("ctx")
    head = lax.axis_index("ctx")
    span = tokens * members
    start = head * HEAD_DIM
    own_keys = lax.dynamic_slice_in_dim(mem_keys, start, HEAD_DIM, 1)
    own_values = lax.dynamic_slice_in_dim(mem_values, start, HEAD_DIM, 1)
    all_keys = lax.all_gather(own_keys, "mem", axis=0, tiled=True)
    all_values = lax.all_gather(own_values, "mem", axis=0, tiled=True)
    ids = lax.all_gather(block_ids, "ctx", axis=0, tiled=True)
    packed = jnp.concatenate(
        [
            queries.reshape(tokens, members, LANES),
            local_keys.reshape(tokens, members, HEAD_DIM),
            local_values.reshape(tokens, members, HEAD_DIM),
        ],
        axis=2,
    )
    packed = jnp.transpose(packed, (1, 0, 2))
    qkv = lax.all_to_all(packed, "ctx", split_axis=0, concat_axis=0, tiled=True)
    qkv = qkv.reshape(span, LANES + 2 * HEAD_DIM)
    vmem = pl.BlockSpec(memory_space=pltpu.VMEM)
    smem = pl.BlockSpec(memory_space=pltpu.SMEM)
    local_out = pl.pallas_call(
        local_kernel,
        out_shape=jax.ShapeDtypeStruct((span, LANES), jnp.float32),
        in_specs=[vmem],
        out_specs=vmem,
        cost_estimate=pl.CostEstimate(
            flops=4 * span * LANES * span, bytes_accessed=2 << 20, transcendentals=span * span * 4
        ),
    )(qkv)
    mixed = pl.pallas_call(
        memory_kernel,
        out_shape=jax.ShapeDtypeStruct((span, LANES), jnp.bfloat16),
        in_specs=[smem, smem, vmem, vmem, vmem, vmem],
        out_specs=vmem,
        cost_estimate=pl.CostEstimate(
            flops=4 * span * LANES * TOPB * BLOCK,
            bytes_accessed=7 << 20,
            transcendentals=span * GROUPS * TOPB * BLOCK,
        ),
    )(ids, gate_bias, qkv, all_keys, all_values, local_out)
    back = lax.all_to_all(
        mixed.reshape(members, tokens, LANES), "ctx", split_axis=0, concat_axis=0, tiled=True
    )
    return jnp.transpose(back, (1, 0, 2)).reshape(tokens, HEADS * HEAD_DIM)


def solution(mesh):
    return jax.shard_map(
        body,
        mesh=mesh,
        in_specs=(
            P(("mem", "ctx"), None),
            P(("mem", "ctx"), None),
            P(("mem", "ctx"), None),
            P("mem", None),
            P("mem", None),
            P(("mem", "ctx"), None),
            P(),
        ),
        out_specs=P(("mem", "ctx"), None),
        check_vma=False,
    )
```

```python
import functools

import jax
import jax.numpy as jnp
from jax import lax
from jax.experimental import pallas as pl
from jax.experimental.pallas import tpu as pltpu
from jax.sharding import PartitionSpec as P

HEADS = 32
KV_HEADS = 8
GROUPS = HEADS // KV_HEADS
HEAD_DIM = 128
BLOCK = 32
TOPB = 16
QBLOCK = 16
LANES = GROUPS * HEAD_DIM
EXP2_SCALE = HEAD_DIM ** (-0.5) * 1.4426950408889634
NEG = -1e30
TILE = 128


def product(left, right, contract_right):
    return lax.dot_general(
        left, right, (((1,), (contract_right,)), ((), ())), preferred_element_type=jnp.float32
    )


def softmax_parts(scores):
    top = jnp.max(scores, axis=-1, keepdims=True)
    weights = jnp.exp2((scores - top) * EXP2_SCALE)
    return weights, jnp.sum(weights, axis=-1, keepdims=True)


def heads_to_rows(rows):
    return jnp.concatenate(
        [rows[:, h * HEAD_DIM : (h + 1) * HEAD_DIM] for h in range(GROUPS)], axis=0
    )


def local_kernel(qkv_ref, out_ref):
    span = qkv_ref.shape[0]
    for tile in range(span // TILE):
        lo, hi = tile * TILE, (tile + 1) * TILE
        query = heads_to_rows(qkv_ref[lo:hi, :LANES])
        keys = qkv_ref[:hi, LANES : LANES + HEAD_DIM]
        values = qkv_ref[:hi, LANES + HEAD_DIM : LANES + 2 * HEAD_DIM]
        scores = product(query, keys, 1)
        row = lax.broadcasted_iota(jnp.int32, scores.shape, 0) % TILE + lo
        col = lax.broadcasted_iota(jnp.int32, scores.shape, 1)
        scores = jnp.where(col <= row, scores, NEG)
        weights, total = softmax_parts(scores)
        summed = product(weights.astype(jnp.bfloat16), values, 0) / total
        for h in range(GROUPS):
            out_ref[lo:hi, h * HEAD_DIM : (h + 1) * HEAD_DIM] = summed[
                h * TILE : (h + 1) * TILE
            ]


def memory_kernel(starts_ref, bias_ref, qkv_ref, local_ref, *refs):
    chunks, (out_ref, store_ref, sems) = refs[:-3], refs[-3:]
    copies, row = [], 0
    for i, chunk in enumerate(chunks):
        rows = chunk.shape[0]
        copies.append(
            pltpu.make_async_copy(chunk, store_ref.at[pl.ds(row, rows)], sems.at[i])
        )
        copies[-1].start()
        row += rows
    head = lax.axis_index("ctx")
    gates = [
        jax.nn.sigmoid(jnp.full((1, HEAD_DIM), bias_ref[head * GROUPS + h], jnp.float32))
        for h in range(GROUPS)
    ]
    query_blocks = qkv_ref.shape[0] // QBLOCK
    for copy in copies:
        copy.wait()

    def one_block(index, carry):
        lo = pl.multiple_of(index * QBLOCK, QBLOCK)
        query = heads_to_rows(qkv_ref[pl.ds(lo, QBLOCK), :LANES])
        starts = [pl.multiple_of(starts_ref[index, j], BLOCK) for j in range(TOPB)]
        keys = jnp.concatenate(
            [store_ref[pl.ds(s, BLOCK), :HEAD_DIM] for s in starts], axis=0
        )
        values = jnp.concatenate(
            [store_ref[pl.ds(s, BLOCK), HEAD_DIM:] for s in starts], axis=0
        )
        weights, total = softmax_parts(product(query, keys, 1))
        summed = product(weights.astype(jnp.bfloat16), values, 0) / total
        for h in range(GROUPS):
            lanes = slice(h * HEAD_DIM, (h + 1) * HEAD_DIM)
            local_out = local_ref[pl.ds(lo, QBLOCK), lanes]
            mixed = gates[h] * summed[h * QBLOCK : (h + 1) * QBLOCK] + (1.0 - gates[h]) * local_out
            out_ref[pl.ds(lo, QBLOCK), lanes] = mixed.astype(jnp.bfloat16)
        return carry

    lax.fori_loop(0, query_blocks, one_block, 0, unroll=2)


BOTH = ("mem", "ctx")
SIDE = 8
CTX = 8


def device(z, y, ctx):
    return (z * SIDE + y) * CTX + ctx


def ring_of(ctx):
    return ctx % 2


def first_groups():
    groups = []
    for ctx in range(CTX):
        for other in range(SIDE):
            if ring_of(ctx) == 0:
                groups.append([device(z, other, ctx) for z in range(SIDE)])
            else:
                groups.append([device(other, y, ctx) for y in range(SIDE)])
    return groups


def shifted(value, step):
    pairs = []
    for z in range(SIDE):
        for y in range(SIDE):
            for ctx in range(CTX):
                if ring_of(ctx) == 0:
                    target = device(z, (y + step) % SIDE, ctx)
                else:
                    target = device((z + step) % SIDE, y, ctx)
                pairs.append((device(z, y, ctx), target))
    return lax.ppermute(value, BOTH, pairs)


def gathered(own):
    rows = own.shape[0]
    spread = jnp.broadcast_to(own[None], (SIDE,) + own.shape)
    chunk = lax.all_to_all(
        spread, BOTH, split_axis=0, concat_axis=0, tiled=True, axis_index_groups=first_groups()
    ).reshape(SIDE * rows, own.shape[1])
    ahead, behind = [chunk], [chunk]
    for _ in range(SIDE // 2 - 1):
        ahead.append(shifted(ahead[-1], 1))
        behind.append(shifted(behind[-1], -1))
    half = chunk.shape[0] // 2
    last_ahead = shifted(ahead[-1][:half], 1)
    last_behind = shifted(behind[-1][half:], -1)
    return ahead + [last_ahead, last_behind] + behind[:0:-1]


def block_rows(ids, held, rows):
    holder, slot = ids // held, ids % held
    z, y = holder // SIDE, holder % SIDE
    mem = lax.axis_index("mem")
    own_z, own_y = mem // SIDE, mem % SIDE
    first = ring_of(lax.axis_index("ctx")) == 0
    back = jnp.where(first, own_y - y, own_z - z) % SIDE
    inner = jnp.where(first, z, y)
    return (back * SIDE + inner) * rows + slot * BLOCK


def body(queries, local_keys, local_values, mem_keys, mem_values, block_ids, gate_bias):
    tokens = queries.shape[0]
    members = lax.axis_size("ctx")
    head = lax.axis_index("ctx")
    span = tokens * members
    rows = mem_keys.shape[0]
    start = head * HEAD_DIM
    own = jnp.concatenate(
        [
            lax.dynamic_slice_in_dim(mem_keys, start, HEAD_DIM, 1),
            lax.dynamic_slice_in_dim(mem_values, start, HEAD_DIM, 1),
        ],
        axis=1,
    )
    chunks = gathered(own)
    id_lanes = jnp.broadcast_to(
        block_ids.reshape(tokens, 1, 1).astype(jnp.bfloat16), (tokens, members, HEAD_DIM)
    )
    packed = jnp.concatenate(
        [
            queries.reshape(tokens, members, LANES),
            local_keys.reshape(tokens, members, HEAD_DIM),
            local_values.reshape(tokens, members, HEAD_DIM),
            id_lanes,
        ],
        axis=2,
    )
    packed = jnp.transpose(packed, (1, 0, 2))
    qkv = lax.all_to_all(packed, "ctx", split_axis=0, concat_axis=0, tiled=True)
    qkv = qkv.reshape(span, LANES + 3 * HEAD_DIM)
    ids = qkv[:, LANES + 2 * HEAD_DIM].astype(jnp.int32).reshape(span // QBLOCK, TOPB)
    starts = block_rows(ids, rows // BLOCK, rows)
    vmem = pl.BlockSpec(memory_space=pltpu.VMEM)
    smem = pl.BlockSpec(memory_space=pltpu.SMEM)
    hbm = pl.BlockSpec(memory_space=pl.ANY)
    local_out = pl.pallas_call(
        local_kernel,
        out_shape=jax.ShapeDtypeStruct((span, LANES), jnp.float32),
        in_specs=[vmem],
        out_specs=vmem,
        cost_estimate=pl.CostEstimate(
            flops=4 * span * LANES * span, bytes_accessed=2 << 20, transcendentals=span * span * 4
        ),
    )(qkv)
    mixed = pl.pallas_call(
        memory_kernel,
        out_shape=jax.ShapeDtypeStruct((span, LANES), jnp.bfloat16),
        in_specs=[smem, smem, vmem, vmem] + [hbm] * len(chunks),
        out_specs=vmem,
        scratch_shapes=[
            pltpu.VMEM((SIDE * SIDE * rows, 2 * HEAD_DIM), jnp.bfloat16),
            pltpu.SemaphoreType.DMA((len(chunks),)),
        ],
        cost_estimate=pl.CostEstimate(
            flops=4 * span * LANES * TOPB * BLOCK,
            bytes_accessed=7 << 20,
            transcendentals=span * GROUPS * TOPB * BLOCK,
        ),
    )(starts, gate_bias, qkv, local_out, *chunks)
    back = lax.all_to_all(
        mixed.reshape(members, tokens, LANES), "ctx", split_axis=0, concat_axis=0, tiled=True
    )
    return jnp.transpose(back, (1, 0, 2)).reshape(tokens, HEADS * HEAD_DIM)


def solution(mesh):
    return jax.shard_map(
        body,
        mesh=mesh,
        in_specs=(
            P(("mem", "ctx"), None),
            P(("mem", "ctx"), None),
            P(("mem", "ctx"), None),
            P("mem", None),
            P("mem", None),
            P(("mem", "ctx"), None),
            P(),
        ),
        out_specs=P(("mem", "ctx"), None),
        check_vma=False,
    )
```

```python
import functools

import jax
import jax.numpy as jnp
from jax import lax
from jax.experimental import pallas as pl
from jax.experimental.pallas import tpu as pltpu
from jax.sharding import PartitionSpec as P

HEADS = 32
KV_HEADS = 8
GROUPS = HEADS // KV_HEADS
HEAD_DIM = 128
BLOCK = 32
TOPB = 16
QBLOCK = 16
LANES = GROUPS * HEAD_DIM
EXP2_SCALE = HEAD_DIM ** (-0.5) * 1.4426950408889634
NEG = -1e30
TILE = 128
TOGETHER = 8


def product(left, right, contract_right):
    return lax.dot_general(
        left, right, (((1,), (contract_right,)), ((), ())), preferred_element_type=jnp.float32
    )


def softmax_parts(scores):
    top = jnp.max(scores, axis=-1, keepdims=True)
    weights = jnp.exp2((scores - top) * EXP2_SCALE)
    return weights, jnp.sum(weights, axis=-1, keepdims=True)


def heads_to_rows(rows):
    return jnp.concatenate(
        [rows[:, h * HEAD_DIM : (h + 1) * HEAD_DIM] for h in range(GROUPS)], axis=0
    )


def pack_kernel(
    ids_ref, queries_ref, keys_ref, values_ref, mem_keys_ref, mem_values_ref, out_ref, own_ref, id_ref
):
    for block in range(ids_ref.shape[0]):
        for j in range(TOPB):
            value = ids_ref[block, j].astype(jnp.float32)
            id_ref[block * TOPB + j : block * TOPB + j + 1, :] = jnp.full(
                (1, HEAD_DIM), value, jnp.float32
            )
    id_lanes = id_ref[...].astype(jnp.bfloat16)
    for head in range(KV_HEADS):
        here = slice(head * HEAD_DIM, (head + 1) * HEAD_DIM)
        out_ref[head, :, :LANES] = queries_ref[:, head * LANES : (head + 1) * LANES]
        out_ref[head, :, LANES : LANES + HEAD_DIM] = keys_ref[:, here]
        out_ref[head, :, LANES + HEAD_DIM : LANES + 2 * HEAD_DIM] = values_ref[:, here]
        out_ref[head, :, LANES + 2 * HEAD_DIM :] = id_lanes
    start = pl.multiple_of(lax.axis_index("ctx") * HEAD_DIM, HEAD_DIM)
    keys = mem_keys_ref[:, pl.ds(start, HEAD_DIM)]
    values = mem_values_ref[:, pl.ds(start, HEAD_DIM)]
    for place in range(own_ref.shape[0]):
        own_ref[place, :, :HEAD_DIM] = keys
        own_ref[place, :, HEAD_DIM:] = values


def local_kernel(qkv_ref, out_ref):
    span = qkv_ref.shape[0]
    for tile in range(span // TILE):
        lo, hi = tile * TILE, (tile + 1) * TILE
        query = heads_to_rows(qkv_ref[lo:hi, :LANES])
        keys = qkv_ref[:hi, LANES : LANES + HEAD_DIM]
        values = qkv_ref[:hi, LANES + HEAD_DIM : LANES + 2 * HEAD_DIM]
        scores = product(query, keys, 1)
        row = lax.broadcasted_iota(jnp.int32, scores.shape, 0) % TILE + lo
        col = lax.broadcasted_iota(jnp.int32, scores.shape, 1)
        scores = jnp.where(col <= row, scores, NEG)
        weights, total = softmax_parts(scores)
        summed = product(weights.astype(jnp.bfloat16), values, 0) / total
        for h in range(GROUPS):
            out_ref[lo:hi, h * HEAD_DIM : (h + 1) * HEAD_DIM] = summed[
                h * TILE : (h + 1) * TILE
            ]


def picked(store_ref, rows, lanes):
    return jnp.concatenate([store_ref[pl.ds(row, BLOCK), lanes] for row in rows], axis=0)


def memory_kernel(starts_ref, bias_ref, qkv_ref, local_ref, *refs):
    chunks, (out_ref, store_ref, sems) = refs[:-3], refs[-3:]
    copies, row = [], 0
    for i, chunk in enumerate(chunks):
        rows = chunk.shape[0]
        copies.append(
            pltpu.make_async_copy(chunk, store_ref.at[pl.ds(row, rows)], sems.at[i])
        )
        copies[-1].start()
        row += rows
    head = lax.axis_index("ctx")
    gates = [
        jax.nn.sigmoid(jnp.full((1, HEAD_DIM), bias_ref[head * GROUPS + h], jnp.float32))
        for h in range(GROUPS)
    ]
    query_blocks = qkv_ref.shape[0] // QBLOCK
    for copy in copies:
        copy.wait()

    def some_blocks(step, carry):
        indices = [step * TOGETHER + k for k in range(TOGETHER)]
        places = [pl.multiple_of(index * QBLOCK, QBLOCK) for index in indices]
        starts = [
            [pl.multiple_of(starts_ref[index, j], BLOCK) for j in range(TOPB)] for index in indices
        ]
        scores = []
        for lo, rows in zip(places, starts):
            query = heads_to_rows(qkv_ref[pl.ds(lo, QBLOCK), :LANES])
            scores.append(product(query, picked(store_ref, rows, slice(0, HEAD_DIM)), 1))
        tops = [jnp.max(score, axis=-1, keepdims=True) for score in scores]
        weights = [jnp.exp2((score - top) * EXP2_SCALE) for score, top in zip(scores, tops)]
        totals = [jnp.sum(weight, axis=-1, keepdims=True) for weight in weights]
        summed = [
            product(
                weight.astype(jnp.bfloat16),
                picked(store_ref, rows, slice(HEAD_DIM, 2 * HEAD_DIM)),
                0,
            )
            for weight, rows in zip(weights, starts)
        ]
        for lo, total, value in zip(places, totals, summed):
            for h in range(GROUPS):
                lanes = slice(h * HEAD_DIM, (h + 1) * HEAD_DIM)
                rows = slice(h * QBLOCK, (h + 1) * QBLOCK)
                memory_out = value[rows] * (gates[h] / total[rows])
                mixed = memory_out + (1.0 - gates[h]) * local_ref[pl.ds(lo, QBLOCK), lanes]
                out_ref[pl.ds(lo, QBLOCK), lanes] = mixed.astype(jnp.bfloat16)
        return carry

    lax.fori_loop(0, query_blocks // TOGETHER, some_blocks, 0)


BOTH = ("mem", "ctx")
SIDE = 8
CTX = 8


def device(z, y, ctx):
    return (z * SIDE + y) * CTX + ctx


def ring_of(ctx):
    return ctx % 2


def first_groups():
    groups = []
    for ctx in range(CTX):
        for other in range(SIDE):
            if ring_of(ctx) == 0:
                groups.append([device(z, other, ctx) for z in range(SIDE)])
            else:
                groups.append([device(other, y, ctx) for y in range(SIDE)])
    return groups


def shifted(value, step):
    pairs = []
    for z in range(SIDE):
        for y in range(SIDE):
            for ctx in range(CTX):
                if ring_of(ctx) == 0:
                    target = device(z, (y + step) % SIDE, ctx)
                else:
                    target = device((z + step) % SIDE, y, ctx)
                pairs.append((device(z, y, ctx), target))
    return lax.ppermute(value, BOTH, pairs)


def gathered(chunk):
    half = chunk.shape[0] // 2
    ahead2, behind2 = shifted(chunk, 2), shifted(chunk, -2)
    ahead1, behind1 = shifted(chunk, 1), shifted(chunk, -1)
    ahead3, behind3 = shifted(ahead2, 1), shifted(behind2, -1)
    ahead4, behind4 = shifted(ahead2[:half], 2), shifted(behind2[half:], -2)
    return [chunk, ahead1, ahead2, ahead3, ahead4, behind4, behind3, behind2, behind1]


def block_rows(ids, held, rows):
    holder, slot = ids // held, ids % held
    z, y = holder // SIDE, holder % SIDE
    mem = lax.axis_index("mem")
    own_z, own_y = mem // SIDE, mem % SIDE
    first = ring_of(lax.axis_index("ctx")) == 0
    back = jnp.where(first, own_y - y, own_z - z) % SIDE
    inner = jnp.where(first, z, y)
    return (back * SIDE + inner) * rows + slot * BLOCK


def body(queries, local_keys, local_values, mem_keys, mem_values, block_ids, gate_bias):
    tokens = queries.shape[0]
    members = lax.axis_size("ctx")
    span = tokens * members
    rows = mem_keys.shape[0]
    vmem = pl.BlockSpec(memory_space=pltpu.VMEM)
    smem = pl.BlockSpec(memory_space=pltpu.SMEM)
    hbm = pl.BlockSpec(memory_space=pl.ANY)
    packed, spread = pl.pallas_call(
        pack_kernel,
        out_shape=(
            jax.ShapeDtypeStruct((members, tokens, LANES + 3 * HEAD_DIM), jnp.bfloat16),
            jax.ShapeDtypeStruct((SIDE, rows, 2 * HEAD_DIM), jnp.bfloat16),
        ),
        in_specs=[smem] + [vmem] * 5,
        out_specs=(vmem, vmem),
        scratch_shapes=[pltpu.VMEM((tokens, HEAD_DIM), jnp.float32)],
        cost_estimate=pl.CostEstimate(flops=0, bytes_accessed=4 << 20, transcendentals=0),
    )(block_ids, queries, local_keys, local_values, mem_keys, mem_values)
    qkv = lax.all_to_all(packed, "ctx", split_axis=0, concat_axis=0, tiled=True)
    qkv = qkv.reshape(span, LANES + 3 * HEAD_DIM)
    chunk = lax.all_to_all(
        spread, BOTH, split_axis=0, concat_axis=0, tiled=True, axis_index_groups=first_groups()
    ).reshape(SIDE * rows, 2 * HEAD_DIM)
    chunks = gathered(chunk)
    ids = qkv[:, LANES + 2 * HEAD_DIM].astype(jnp.int32).reshape(span // QBLOCK, TOPB)
    starts = block_rows(ids, rows // BLOCK, rows)
    local_out = pl.pallas_call(
        local_kernel,
        out_shape=jax.ShapeDtypeStruct((span, LANES), jnp.float32),
        in_specs=[vmem],
        out_specs=vmem,
        cost_estimate=pl.CostEstimate(
            flops=4 * span * LANES * span, bytes_accessed=2 << 20, transcendentals=span * span * 4
        ),
    )(qkv)
    mixed = pl.pallas_call(
        memory_kernel,
        out_shape=jax.ShapeDtypeStruct((span, LANES), jnp.bfloat16),
        in_specs=[smem, smem, vmem, vmem] + [hbm] * len(chunks),
        out_specs=vmem,
        scratch_shapes=[
            pltpu.VMEM((SIDE * SIDE * rows, 2 * HEAD_DIM), jnp.bfloat16),
            pltpu.SemaphoreType.DMA((len(chunks),)),
        ],
        cost_estimate=pl.CostEstimate(
            flops=4 * span * LANES * TOPB * BLOCK,
            bytes_accessed=7 << 20,
            transcendentals=span * GROUPS * TOPB * BLOCK,
        ),
    )(starts, gate_bias, qkv, local_out, *chunks)
    back = lax.all_to_all(
        mixed.reshape(members, tokens, LANES), "ctx", split_axis=0, concat_axis=0, tiled=True
    )
    return jnp.transpose(back, (1, 0, 2)).reshape(tokens, HEADS * HEAD_DIM)


def solution(mesh):
    return jax.shard_map(
        body,
        mesh=mesh,
        in_specs=(
            P(("mem", "ctx"), None),
            P(("mem", "ctx"), None),
            P(("mem", "ctx"), None),
            P("mem", None),
            P("mem", None),
            P(("mem", "ctx"), None),
            P(),
        ),
        out_specs=P(("mem", "ctx"), None),
        check_vma=False,
    )
```

```python
import functools

import jax
import jax.numpy as jnp
from jax import lax
from jax.experimental import pallas as pl
from jax.experimental.pallas import tpu as pltpu
from jax.sharding import PartitionSpec as P

HEADS = 32
KV_HEADS = 8
GROUPS = HEADS // KV_HEADS
HEAD_DIM = 128
BLOCK = 32
TOPB = 16
QBLOCK = 16
LANES = GROUPS * HEAD_DIM
EXP2_SCALE = HEAD_DIM ** (-0.5) * 1.4426950408889634
NEG = -1e30
TILE = 128
TOGETHER = 8


def product(left, right, contract_right):
    return lax.dot_general(
        left, right, (((1,), (contract_right,)), ((), ())), preferred_element_type=jnp.float32
    )


def softmax_parts(scores):
    top = jnp.max(scores, axis=-1, keepdims=True)
    weights = jnp.exp2((scores - top) * EXP2_SCALE)
    return weights, jnp.sum(weights, axis=-1, keepdims=True)


def heads_to_rows(rows):
    return jnp.concatenate(
        [rows[:, h * HEAD_DIM : (h + 1) * HEAD_DIM] for h in range(GROUPS)], axis=0
    )


def pack_kernel(
    ids_ref, queries_ref, keys_ref, values_ref, mem_keys_ref, mem_values_ref, out_ref, own_ref, id_ref
):
    for block in range(ids_ref.shape[0]):
        for j in range(TOPB):
            value = ids_ref[block, j].astype(jnp.float32)
            id_ref[block * TOPB + j : block * TOPB + j + 1, :] = jnp.full(
                (1, HEAD_DIM), value, jnp.float32
            )
    id_lanes = id_ref[...].astype(jnp.bfloat16)
    for head in range(KV_HEADS):
        here = slice(head * HEAD_DIM, (head + 1) * HEAD_DIM)
        out_ref[head, :, :LANES] = queries_ref[:, head * LANES : (head + 1) * LANES]
        out_ref[head, :, LANES : LANES + HEAD_DIM] = keys_ref[:, here]
        out_ref[head, :, LANES + HEAD_DIM : LANES + 2 * HEAD_DIM] = values_ref[:, here]
        out_ref[head, :, LANES + 2 * HEAD_DIM :] = id_lanes
    start = pl.multiple_of(lax.axis_index("ctx") * HEAD_DIM, HEAD_DIM)
    keys = mem_keys_ref[:, pl.ds(start, HEAD_DIM)]
    values = mem_values_ref[:, pl.ds(start, HEAD_DIM)]
    for place in range(own_ref.shape[0]):
        own_ref[place, :, :HEAD_DIM] = keys
        own_ref[place, :, HEAD_DIM:] = values


def local_kernel(qkv_ref, out_ref):
    span = qkv_ref.shape[0]
    for tile in range(span // TILE):
        lo, hi = tile * TILE, (tile + 1) * TILE
        query = heads_to_rows(qkv_ref[lo:hi, :LANES])
        keys = qkv_ref[:hi, LANES : LANES + HEAD_DIM]
        values = qkv_ref[:hi, LANES + HEAD_DIM : LANES + 2 * HEAD_DIM]
        scores = product(query, keys, 1)
        row = lax.broadcasted_iota(jnp.int32, scores.shape, 0) % TILE + lo
        col = lax.broadcasted_iota(jnp.int32, scores.shape, 1)
        scores = jnp.where(col <= row, scores, NEG)
        weights, total = softmax_parts(scores)
        summed = product(weights.astype(jnp.bfloat16), values, 0) / total
        for h in range(GROUPS):
            out_ref[lo:hi, h * HEAD_DIM : (h + 1) * HEAD_DIM] = summed[
                h * TILE : (h + 1) * TILE
            ]


def picked(store_ref, rows, lanes):
    return jnp.concatenate([store_ref[pl.ds(row, BLOCK), lanes] for row in rows], axis=0)


def memory_kernel(starts_ref, bias_ref, qkv_ref, local_ref, *refs):
    chunks, (out_ref, store_ref, sems) = refs[:-3], refs[-3:]
    copies, row = [], 0
    for i, chunk in enumerate(chunks):
        rows = chunk.shape[0]
        copies.append(
            pltpu.make_async_copy(chunk, store_ref.at[pl.ds(row, rows)], sems.at[i])
        )
        copies[-1].start()
        row += rows
    head = lax.axis_index("ctx")
    gates = [
        jax.nn.sigmoid(jnp.full((1, HEAD_DIM), bias_ref[head * GROUPS + h], jnp.float32))
        for h in range(GROUPS)
    ]
    query_blocks = qkv_ref.shape[0] // QBLOCK
    for copy in copies:
        copy.wait()

    def some_blocks(step, carry):
        indices = [step * TOGETHER + k for k in range(TOGETHER)]
        places = [pl.multiple_of(index * QBLOCK, QBLOCK) for index in indices]
        starts = [
            [pl.multiple_of(starts_ref[index, j], BLOCK) for j in range(TOPB)] for index in indices
        ]
        scores = []
        for lo, rows in zip(places, starts):
            query = heads_to_rows(qkv_ref[pl.ds(lo, QBLOCK), :LANES])
            scores.append(product(query, picked(store_ref, rows, slice(0, HEAD_DIM)), 1))
        tops = [jnp.max(score, axis=-1, keepdims=True) for score in scores]
        weights = [jnp.exp2((score - top) * EXP2_SCALE) for score, top in zip(scores, tops)]
        totals = [jnp.sum(weight, axis=-1, keepdims=True) for weight in weights]
        summed = [
            product(
                weight.astype(jnp.bfloat16),
                picked(store_ref, rows, slice(HEAD_DIM, 2 * HEAD_DIM)),
                0,
            )
            for weight, rows in zip(weights, starts)
        ]
        for lo, total, value in zip(places, totals, summed):
            for h in range(GROUPS):
                lanes = slice(h * HEAD_DIM, (h + 1) * HEAD_DIM)
                rows = slice(h * QBLOCK, (h + 1) * QBLOCK)
                memory_out = value[rows] * (gates[h] / total[rows])
                mixed = memory_out + (1.0 - gates[h]) * local_ref[pl.ds(lo, QBLOCK), lanes]
                out_ref[pl.ds(lo, QBLOCK), lanes] = mixed.astype(jnp.bfloat16)
        return carry

    lax.fori_loop(0, query_blocks // TOGETHER, some_blocks, 0)


BOTH = ("mem", "ctx")
SIDE = 8
CTX = 8
SLOPE = 3


def device(along, across, ctx):
    z, y = (across, along) if ctx % 2 == 0 else (along, across)
    return (z * SIDE + y) * CTX + ctx


def colour(along, across):
    return (along + SLOPE * across) % SIDE


def colour_groups():
    return [
        [device((wanted - SLOPE * across) % SIDE, across, ctx) for across in range(SIDE)]
        for ctx in range(CTX)
        for wanted in range(SIDE)
    ]


def shifted(value, along_step, across_step):
    pairs = [
        (
            device(along, across, ctx),
            device((along + along_step) % SIDE, (across + across_step) % SIDE, ctx),
        )
        for along in range(SIDE)
        for across in range(SIDE)
        for ctx in range(CTX)
    ]
    return lax.ppermute(value, BOTH, pairs)


def gathered(chunk):
    back1, back7 = shifted(chunk, 1, 0), shifted(chunk, -1, 0)
    back3, back5 = shifted(chunk, 0, 1), shifted(chunk, 0, -1)
    back2, back6 = shifted(back1, 1, 0), shifted(back7, -1, 0)
    back4 = shifted(back1, 0, 1)
    return [chunk, back1, back2, back3, back4, back5, back6, back7]


def block_rows(ids, held, rows):
    holder, slot = ids // held, ids % held
    mem = lax.axis_index("mem")
    first = lax.axis_index("ctx") % 2 == 0

    def position(index):
        z, y = index // SIDE, index % SIDE
        return jnp.where(first, y, z), jnp.where(first, z, y)

    along, across = position(holder)
    back = (colour(*position(mem)) - colour(along, across)) % SIDE
    return (back * SIDE + across) * rows + slot * BLOCK


def body(queries, local_keys, local_values, mem_keys, mem_values, block_ids, gate_bias):
    tokens = queries.shape[0]
    members = lax.axis_size("ctx")
    span = tokens * members
    rows = mem_keys.shape[0]
    vmem = pl.BlockSpec(memory_space=pltpu.VMEM)
    smem = pl.BlockSpec(memory_space=pltpu.SMEM)
    hbm = pl.BlockSpec(memory_space=pl.ANY)
    packed, spread = pl.pallas_call(
        pack_kernel,
        out_shape=(
            jax.ShapeDtypeStruct((members, tokens, LANES + 3 * HEAD_DIM), jnp.bfloat16),
            jax.ShapeDtypeStruct((SIDE, rows, 2 * HEAD_DIM), jnp.bfloat16),
        ),
        in_specs=[smem] + [vmem] * 5,
        out_specs=(vmem, vmem),
        scratch_shapes=[pltpu.VMEM((tokens, HEAD_DIM), jnp.float32)],
        cost_estimate=pl.CostEstimate(flops=0, bytes_accessed=4 << 20, transcendentals=0),
    )(block_ids, queries, local_keys, local_values, mem_keys, mem_values)
    qkv = lax.all_to_all(packed, "ctx", split_axis=0, concat_axis=0, tiled=True)
    qkv = qkv.reshape(span, LANES + 3 * HEAD_DIM)
    chunk = lax.all_to_all(
        spread, BOTH, split_axis=0, concat_axis=0, tiled=True, axis_index_groups=colour_groups()
    ).reshape(SIDE * rows, 2 * HEAD_DIM)
    chunks = gathered(chunk)
    ids = qkv[:, LANES + 2 * HEAD_DIM].astype(jnp.int32).reshape(span // QBLOCK, TOPB)
    starts = block_rows(ids, rows // BLOCK, rows)
    local_out = pl.pallas_call(
        local_kernel,
        out_shape=jax.ShapeDtypeStruct((span, LANES), jnp.float32),
        in_specs=[vmem],
        out_specs=vmem,
        cost_estimate=pl.CostEstimate(
            flops=4 * span * LANES * span, bytes_accessed=2 << 20, transcendentals=span * span * 4
        ),
    )(qkv)
    mixed = pl.pallas_call(
        memory_kernel,
        out_shape=jax.ShapeDtypeStruct((span, LANES), jnp.bfloat16),
        in_specs=[smem, smem, vmem, vmem] + [hbm] * len(chunks),
        out_specs=vmem,
        scratch_shapes=[
            pltpu.VMEM((SIDE * SIDE * rows, 2 * HEAD_DIM), jnp.bfloat16),
            pltpu.SemaphoreType.DMA((len(chunks),)),
        ],
        cost_estimate=pl.CostEstimate(
            flops=4 * span * LANES * TOPB * BLOCK,
            bytes_accessed=7 << 20,
            transcendentals=span * GROUPS * TOPB * BLOCK,
        ),
    )(starts, gate_bias, qkv, local_out, *chunks)
    back = lax.all_to_all(
        mixed.reshape(members, tokens, LANES), "ctx", split_axis=0, concat_axis=0, tiled=True
    )
    return jnp.transpose(back, (1, 0, 2)).reshape(tokens, HEADS * HEAD_DIM)


def solution(mesh):
    return jax.shard_map(
        body,
        mesh=mesh,
        in_specs=(
            P(("mem", "ctx"), None),
            P(("mem", "ctx"), None),
            P(("mem", "ctx"), None),
            P("mem", None),
            P("mem", None),
            P(("mem", "ctx"), None),
            P(),
        ),
        out_specs=P(("mem", "ctx"), None),
        check_vma=False,
    )
```

```python
import functools

import jax
import jax.numpy as jnp
from jax import lax
from jax.experimental import pallas as pl
from jax.experimental.pallas import tpu as pltpu
from jax.sharding import PartitionSpec as P

HEADS = 32
KV_HEADS = 8
GROUPS = HEADS // KV_HEADS
HEAD_DIM = 128
BLOCK = 32
TOPB = 16
QBLOCK = 16
LANES = GROUPS * HEAD_DIM
EXP2_SCALE = HEAD_DIM ** (-0.5) * 1.4426950408889634
NEG = -1e30
TILE = 128
TOGETHER = 32


def product(left, right, contract_right):
    return lax.dot_general(
        left, right, (((1,), (contract_right,)), ((), ())), preferred_element_type=jnp.float32
    )


def softmax_parts(scores):
    top = jnp.max(scores, axis=-1, keepdims=True)
    weights = jnp.exp2((scores - top) * EXP2_SCALE)
    return weights, jnp.sum(weights, axis=-1, keepdims=True)


def heads_to_rows(rows):
    return jnp.concatenate(
        [rows[:, h * HEAD_DIM : (h + 1) * HEAD_DIM] for h in range(GROUPS)], axis=0
    )


def pack_kernel(
    ids_ref, queries_ref, keys_ref, values_ref, mem_keys_ref, mem_values_ref, out_ref, own_ref, id_ref
):
    for block in range(ids_ref.shape[0]):
        for j in range(TOPB):
            value = ids_ref[block, j].astype(jnp.float32)
            id_ref[block * TOPB + j : block * TOPB + j + 1, :] = jnp.full(
                (1, HEAD_DIM), value, jnp.float32
            )
    id_lanes = id_ref[...].astype(jnp.bfloat16)
    for head in range(KV_HEADS):
        here = slice(head * HEAD_DIM, (head + 1) * HEAD_DIM)
        out_ref[head, :, :LANES] = queries_ref[:, head * LANES : (head + 1) * LANES]
        out_ref[head, :, LANES : LANES + HEAD_DIM] = keys_ref[:, here]
        out_ref[head, :, LANES + HEAD_DIM : LANES + 2 * HEAD_DIM] = values_ref[:, here]
        out_ref[head, :, LANES + 2 * HEAD_DIM :] = id_lanes
    start = pl.multiple_of(lax.axis_index("ctx") * HEAD_DIM, HEAD_DIM)
    keys = mem_keys_ref[:, pl.ds(start, HEAD_DIM)]
    values = mem_values_ref[:, pl.ds(start, HEAD_DIM)]
    for place in range(own_ref.shape[0]):
        own_ref[place, :, :HEAD_DIM] = keys
        own_ref[place, :, HEAD_DIM:] = values


def block_rows(ids, held, rows):
    holder, slot = ids // held, ids % held
    z, y = holder // SIDE, holder % SIDE
    mem = lax.axis_index("mem")
    own_z, own_y = mem // SIDE, mem % SIDE
    first = lax.axis_index("ctx") % 2 == 0
    back = (jnp.where(first, own_y - y, own_z - z) + SIDE) % SIDE
    inner = jnp.where(first, z, y)
    return (back * SIDE + inner) * rows + slot * BLOCK


def local_kernel(held, rows, qkv_ref, out_ref, starts_ref):
    span = qkv_ref.shape[0]
    diagonal = lax.broadcasted_iota(jnp.int32, (TILE, HEAD_DIM), 0) == lax.broadcasted_iota(
        jnp.int32, (TILE, HEAD_DIM), 1
    )
    for tile in range(span // TILE):
        ids = qkv_ref[tile * TILE : (tile + 1) * TILE, LANES + 2 * HEAD_DIM :].astype(jnp.float32)
        ids = jnp.sum(jnp.where(diagonal, ids, 0.0), axis=0, keepdims=True).astype(jnp.int32)
        starts_ref[tile : tile + 1, :] = block_rows(ids, held, rows)
    for tile in range(span // TILE):
        lo, hi = tile * TILE, (tile + 1) * TILE
        query = heads_to_rows(qkv_ref[lo:hi, :LANES])
        keys = qkv_ref[:hi, LANES : LANES + HEAD_DIM]
        values = qkv_ref[:hi, LANES + HEAD_DIM : LANES + 2 * HEAD_DIM]
        scores = product(query, keys, 1)
        row = lax.broadcasted_iota(jnp.int32, scores.shape, 0) % TILE + lo
        col = lax.broadcasted_iota(jnp.int32, scores.shape, 1)
        scores = jnp.where(col <= row, scores, NEG)
        weights, total = softmax_parts(scores)
        summed = product(weights.astype(jnp.bfloat16), values, 0) / total
        for h in range(GROUPS):
            out_ref[lo:hi, h * HEAD_DIM : (h + 1) * HEAD_DIM] = summed[
                h * TILE : (h + 1) * TILE
            ]


def picked(store_ref, rows, lanes):
    return jnp.concatenate([store_ref[pl.ds(row, BLOCK), lanes] for row in rows], axis=0)


def memory_kernel(starts_ref, bias_ref, qkv_ref, local_ref, *refs):
    chunks, (out_ref, store_ref, sems) = refs[:-3], refs[-3:]
    copies, row = [], 0
    for i, chunk in enumerate(chunks):
        rows = chunk.shape[0]
        copies.append(
            pltpu.make_async_copy(chunk, store_ref.at[pl.ds(row, rows)], sems.at[i])
        )
        copies[-1].start()
        row += rows
    head = lax.axis_index("ctx")
    gates = [
        jax.nn.sigmoid(jnp.full((1, HEAD_DIM), bias_ref[head * GROUPS + h], jnp.float32))
        for h in range(GROUPS)
    ]
    query_blocks = qkv_ref.shape[0] // QBLOCK
    for copy in copies:
        copy.wait()

    for first in range(0, query_blocks, TOGETHER):
        indices = range(first, first + TOGETHER)
        places = [index * QBLOCK for index in indices]
        starts = [
            [pl.multiple_of(starts_ref[divmod(index * TOPB + j, TILE)], BLOCK) for j in range(TOPB)] for index in indices
        ]
        scores = []
        for lo, rows in zip(places, starts):
            query = heads_to_rows(qkv_ref[pl.ds(lo, QBLOCK), :LANES])
            scores.append(product(query, picked(store_ref, rows, slice(0, HEAD_DIM)), 1))
        tops = [jnp.max(score, axis=-1, keepdims=True) for score in scores]
        weights = [jnp.exp2((score - top) * EXP2_SCALE) for score, top in zip(scores, tops)]
        totals = [jnp.sum(weight, axis=-1, keepdims=True) for weight in weights]
        summed = [
            product(
                weight.astype(jnp.bfloat16),
                picked(store_ref, rows, slice(HEAD_DIM, 2 * HEAD_DIM)),
                0,
            )
            for weight, rows in zip(weights, starts)
        ]
        for lo, total, value in zip(places, totals, summed):
            for h in range(GROUPS):
                lanes = slice(h * HEAD_DIM, (h + 1) * HEAD_DIM)
                rows = slice(h * QBLOCK, (h + 1) * QBLOCK)
                memory_out = value[rows] * (gates[h] / total[rows])
                mixed = memory_out + (1.0 - gates[h]) * local_ref[pl.ds(lo, QBLOCK), lanes]
                out_ref[pl.ds(lo, QBLOCK), lanes] = mixed.astype(jnp.bfloat16)


BOTH = ("mem", "ctx")
SIDE = 8
CTX = 8


def device(z, y, ctx):
    return (z * SIDE + y) * CTX + ctx


def ring_of(ctx):
    return ctx % 2


def first_groups():
    groups = []
    for ctx in range(CTX):
        for other in range(SIDE):
            if ring_of(ctx) == 0:
                groups.append([device(z, other, ctx) for z in range(SIDE)])
            else:
                groups.append([device(other, y, ctx) for y in range(SIDE)])
    return groups


def shifted(value, step):
    pairs = []
    for z in range(SIDE):
        for y in range(SIDE):
            for ctx in range(CTX):
                if ring_of(ctx) == 0:
                    target = device(z, (y + step) % SIDE, ctx)
                else:
                    target = device((z + step) % SIDE, y, ctx)
                pairs.append((device(z, y, ctx), target))
    return lax.ppermute(value, BOTH, pairs)


def gathered(chunk):
    ahead2, behind2 = shifted(chunk, 2), shifted(chunk, -2)
    ahead1, behind1 = shifted(chunk, 1), shifted(chunk, -1)
    ahead4 = shifted(ahead2, 2)
    ahead3, behind3 = shifted(ahead2, 1), shifted(behind2, -1)
    return [chunk, ahead1, ahead2, ahead3, ahead4, behind3, behind2, behind1]


def body(queries, local_keys, local_values, mem_keys, mem_values, block_ids, gate_bias):
    tokens = queries.shape[0]
    members = lax.axis_size("ctx")
    span = tokens * members
    rows = mem_keys.shape[0]
    vmem = pl.BlockSpec(memory_space=pltpu.VMEM)
    smem = pl.BlockSpec(memory_space=pltpu.SMEM)
    hbm = pl.BlockSpec(memory_space=pl.ANY)
    packed, spread = pl.pallas_call(
        pack_kernel,
        out_shape=(
            jax.ShapeDtypeStruct((members, tokens, LANES + 3 * HEAD_DIM), jnp.bfloat16),
            jax.ShapeDtypeStruct((SIDE, rows, 2 * HEAD_DIM), jnp.bfloat16),
        ),
        in_specs=[smem] + [vmem] * 5,
        out_specs=(vmem, vmem),
        scratch_shapes=[pltpu.VMEM((tokens, HEAD_DIM), jnp.float32)],
        cost_estimate=pl.CostEstimate(flops=0, bytes_accessed=4 << 20, transcendentals=0),
    )(block_ids, queries, local_keys, local_values, mem_keys, mem_values)
    qkv = lax.all_to_all(packed, "ctx", split_axis=0, concat_axis=0, tiled=True)
    qkv = qkv.reshape(span, LANES + 3 * HEAD_DIM)
    chunk = lax.all_to_all(
        spread, BOTH, split_axis=0, concat_axis=0, tiled=True, axis_index_groups=first_groups()
    ).reshape(SIDE * rows, 2 * HEAD_DIM)
    chunks = gathered(chunk)
    local_out, starts = pl.pallas_call(
        functools.partial(local_kernel, rows // BLOCK, rows),
        out_shape=(
            jax.ShapeDtypeStruct((span, LANES), jnp.float32),
            jax.ShapeDtypeStruct((span // TILE, TILE), jnp.int32),
        ),
        in_specs=[vmem],
        out_specs=(vmem, vmem),
        cost_estimate=pl.CostEstimate(
            flops=4 * span * LANES * span, bytes_accessed=2 << 20, transcendentals=span * span * 4
        ),
    )(qkv)
    mixed = pl.pallas_call(
        memory_kernel,
        out_shape=jax.ShapeDtypeStruct((span, LANES), jnp.bfloat16),
        in_specs=[smem, smem, vmem, vmem] + [hbm] * len(chunks),
        out_specs=vmem,
        scratch_shapes=[
            pltpu.VMEM((SIDE * SIDE * rows, 2 * HEAD_DIM), jnp.bfloat16),
            pltpu.SemaphoreType.DMA((len(chunks),)),
        ],
        cost_estimate=pl.CostEstimate(
            flops=4 * span * LANES * TOPB * BLOCK,
            bytes_accessed=7 << 20,
            transcendentals=span * GROUPS * TOPB * BLOCK,
        ),
    )(starts, gate_bias, qkv, local_out, *chunks)
    back = lax.all_to_all(
        mixed.reshape(members, tokens, LANES), "ctx", split_axis=0, concat_axis=0, tiled=True
    )
    return jnp.transpose(back, (1, 0, 2)).reshape(tokens, HEADS * HEAD_DIM)


def solution(mesh):
    return jax.shard_map(
        body,
        mesh=mesh,
        in_specs=(
            P(("mem", "ctx"), None),
            P(("mem", "ctx"), None),
            P(("mem", "ctx"), None),
            P("mem", None),
            P("mem", None),
            P(("mem", "ctx"), None),
            P(),
        ),
        out_specs=P(("mem", "ctx"), None),
        check_vma=False,
    )
```

```python
import functools

import jax
import jax.numpy as jnp
from jax import lax
from jax.experimental import pallas as pl
from jax.experimental.pallas import tpu as pltpu
from jax.sharding import PartitionSpec as P

HEADS = 32
KV_HEADS = 8
GROUPS = HEADS // KV_HEADS
HEAD_DIM = 128
BLOCK = 32
TOPB = 16
QBLOCK = 16
LANES = GROUPS * HEAD_DIM
EXP2_SCALE = HEAD_DIM ** (-0.5) * 1.4426950408889634
NEG = -1e30
TILE = 128
TOGETHER = 32


def product(left, right, contract_right):
    return lax.dot_general(
        left, right, (((1,), (contract_right,)), ((), ())), preferred_element_type=jnp.float32
    )


def softmax_parts(scores):
    top = jnp.max(scores, axis=-1, keepdims=True)
    weights = jnp.exp2((scores - top) * EXP2_SCALE)
    return weights, jnp.sum(weights, axis=-1, keepdims=True)


def heads_to_rows(rows):
    return jnp.concatenate(
        [rows[:, h * HEAD_DIM : (h + 1) * HEAD_DIM] for h in range(GROUPS)], axis=0
    )


def pack_kernel(
    ids_ref, queries_ref, keys_ref, values_ref, mem_keys_ref, mem_values_ref, out_ref, own_ref, id_ref
):
    for block in range(ids_ref.shape[0]):
        for j in range(TOPB):
            value = ids_ref[block, j].astype(jnp.float32)
            id_ref[block * TOPB + j : block * TOPB + j + 1, :] = jnp.full(
                (1, HEAD_DIM), value, jnp.float32
            )
    id_lanes = id_ref[...].astype(jnp.bfloat16)
    for head in range(KV_HEADS):
        here = slice(head * HEAD_DIM, (head + 1) * HEAD_DIM)
        out_ref[head, :, :LANES] = queries_ref[:, head * LANES : (head + 1) * LANES]
        out_ref[head, :, LANES : LANES + HEAD_DIM] = keys_ref[:, here]
        out_ref[head, :, LANES + HEAD_DIM : LANES + 2 * HEAD_DIM] = values_ref[:, here]
        out_ref[head, :, LANES + 2 * HEAD_DIM :] = id_lanes
    start = pl.multiple_of(lax.axis_index("ctx") * HEAD_DIM, HEAD_DIM)
    keys = mem_keys_ref[:, pl.ds(start, HEAD_DIM)]
    values = mem_values_ref[:, pl.ds(start, HEAD_DIM)]
    for place in range(own_ref.shape[0]):
        own_ref[place, :, :HEAD_DIM] = keys
        own_ref[place, :, HEAD_DIM:] = values


def block_rows(ids, held, rows):
    holder, slot = ids // held, ids % held
    z, y = holder // SIDE, holder % SIDE
    mem = lax.axis_index("mem")
    own_z, own_y = mem // SIDE, mem % SIDE
    first = lax.axis_index("ctx") % 2 == 0
    back = (jnp.where(first, own_y - y, own_z - z) + SIDE) % SIDE
    inner = jnp.where(first, z, y)
    return (back * SIDE + inner) * rows + slot * BLOCK


def local_kernel(held, rows, qkv_ref, out_ref, starts_ref):
    span = qkv_ref.shape[0]
    diagonal = lax.broadcasted_iota(jnp.int32, (TILE, HEAD_DIM), 0) == lax.broadcasted_iota(
        jnp.int32, (TILE, HEAD_DIM), 1
    )
    for tile in range(span // TILE):
        ids = qkv_ref[tile * TILE : (tile + 1) * TILE, LANES + 2 * HEAD_DIM :].astype(jnp.float32)
        ids = jnp.sum(jnp.where(diagonal, ids, 0.0), axis=0, keepdims=True).astype(jnp.int32)
        starts_ref[tile : tile + 1, :] = block_rows(ids, held, rows)
    for tile in range(span // TILE):
        lo, hi = tile * TILE, (tile + 1) * TILE
        query = heads_to_rows(qkv_ref[lo:hi, :LANES])
        keys = qkv_ref[:hi, LANES : LANES + HEAD_DIM]
        values = qkv_ref[:hi, LANES + HEAD_DIM : LANES + 2 * HEAD_DIM]
        scores = product(query, keys, 1)
        row = lax.broadcasted_iota(jnp.int32, scores.shape, 0) % TILE + lo
        col = lax.broadcasted_iota(jnp.int32, scores.shape, 1)
        scores = jnp.where(col <= row, scores, NEG)
        weights, total = softmax_parts(scores)
        summed = product(weights.astype(jnp.bfloat16), values, 0) / total
        for h in range(GROUPS):
            out_ref[lo:hi, h * HEAD_DIM : (h + 1) * HEAD_DIM] = summed[
                h * TILE : (h + 1) * TILE
            ]


def picked(store_ref, rows, lanes):
    return jnp.concatenate([store_ref[pl.ds(row, BLOCK), lanes] for row in rows], axis=0)


def memory_kernel(starts_ref, bias_ref, qkv_ref, local_ref, *refs):
    chunks, (out_ref, store_ref, sems) = refs[:-3], refs[-3:]
    copies, row = [], 0
    for i, chunk in enumerate(chunks):
        rows = chunk.shape[0]
        copies.append(
            pltpu.make_async_copy(chunk, store_ref.at[pl.ds(row, rows)], sems.at[i])
        )
        copies[-1].start()
        row += rows
    head = lax.axis_index("ctx")
    gates = [
        jax.nn.sigmoid(jnp.full((1, HEAD_DIM), bias_ref[head * GROUPS + h], jnp.float32))
        for h in range(GROUPS)
    ]
    query_blocks = qkv_ref.shape[0] // QBLOCK
    for copy in copies:
        copy.wait()

    for first in range(0, query_blocks, TOGETHER):
        indices = range(first, first + TOGETHER)
        places = [index * QBLOCK for index in indices]
        starts = [
            [pl.multiple_of(starts_ref[divmod(index * TOPB + j, TILE)], BLOCK) for j in range(TOPB)] for index in indices
        ]
        scores = []
        for lo, rows in zip(places, starts):
            query = heads_to_rows(qkv_ref[pl.ds(lo, QBLOCK), :LANES])
            scores.append(product(query, picked(store_ref, rows, slice(0, HEAD_DIM)), 1))
        tops = [jnp.max(score, axis=-1, keepdims=True) for score in scores]
        weights = [jnp.exp2((score - top) * EXP2_SCALE) for score, top in zip(scores, tops)]
        totals = [jnp.sum(weight, axis=-1, keepdims=True) for weight in weights]
        summed = [
            product(
                weight.astype(jnp.bfloat16),
                picked(store_ref, rows, slice(HEAD_DIM, 2 * HEAD_DIM)),
                0,
            )
            for weight, rows in zip(weights, starts)
        ]
        for lo, total, value in zip(places, totals, summed):
            for h in range(GROUPS):
                lanes = slice(h * HEAD_DIM, (h + 1) * HEAD_DIM)
                rows = slice(h * QBLOCK, (h + 1) * QBLOCK)
                memory_out = value[rows] * (gates[h] / total[rows])
                mixed = memory_out + (1.0 - gates[h]) * local_ref[pl.ds(lo, QBLOCK), lanes]
                out_ref[pl.ds(lo, QBLOCK), lanes] = mixed.astype(jnp.bfloat16)


BOTH = ("mem", "ctx")
SIDE = 8
CTX = 8


def device(z, y, ctx):
    return (z * SIDE + y) * CTX + ctx


def ring_of(ctx):
    return ctx % 2


def first_groups():
    groups = []
    for ctx in range(CTX):
        for other in range(SIDE):
            if ring_of(ctx) == 0:
                groups.append([device(z, other, ctx) for z in range(SIDE)])
            else:
                groups.append([device(other, y, ctx) for y in range(SIDE)])
    return groups


def shifted(value, step):
    pairs = []
    for z in range(SIDE):
        for y in range(SIDE):
            for ctx in range(CTX):
                if ring_of(ctx) == 0:
                    target = device(z, (y + step) % SIDE, ctx)
                else:
                    target = device((z + step) % SIDE, y, ctx)
                pairs.append((device(z, y, ctx), target))
    return lax.ppermute(value, BOTH, pairs)


def gathered(chunk):
    ahead2, behind2 = shifted(chunk, 2), shifted(chunk, -2)
    ahead1, behind1 = shifted(chunk, 1), shifted(chunk, -1)
    ahead3, behind3 = shifted(ahead2, 1), shifted(behind2, -1)
    half = chunk.shape[0] // 2
    ahead4, behind4 = shifted(ahead2[:half], 2), shifted(behind2[half:], -2)
    return [chunk, ahead1, ahead2, ahead3, ahead4, behind4, behind3, behind2, behind1]


def body(queries, local_keys, local_values, mem_keys, mem_values, block_ids, gate_bias):
    tokens = queries.shape[0]
    members = lax.axis_size("ctx")
    span = tokens * members
    rows = mem_keys.shape[0]
    vmem = pl.BlockSpec(memory_space=pltpu.VMEM)
    smem = pl.BlockSpec(memory_space=pltpu.SMEM)
    hbm = pl.BlockSpec(memory_space=pl.ANY)
    packed, spread = pl.pallas_call(
        pack_kernel,
        out_shape=(
            jax.ShapeDtypeStruct((members, tokens, LANES + 3 * HEAD_DIM), jnp.bfloat16),
            jax.ShapeDtypeStruct((SIDE, rows, 2 * HEAD_DIM), jnp.bfloat16),
        ),
        in_specs=[smem] + [vmem] * 5,
        out_specs=(vmem, vmem),
        scratch_shapes=[pltpu.VMEM((tokens, HEAD_DIM), jnp.float32)],
        cost_estimate=pl.CostEstimate(flops=0, bytes_accessed=4 << 20, transcendentals=0),
    )(block_ids, queries, local_keys, local_values, mem_keys, mem_values)
    qkv = lax.all_to_all(packed, "ctx", split_axis=0, concat_axis=0, tiled=True)
    qkv = qkv.reshape(span, LANES + 3 * HEAD_DIM)
    chunk = lax.all_to_all(
        spread, BOTH, split_axis=0, concat_axis=0, tiled=True, axis_index_groups=first_groups()
    ).reshape(SIDE * rows, 2 * HEAD_DIM)
    chunks = gathered(chunk)
    local_out, starts = pl.pallas_call(
        functools.partial(local_kernel, rows // BLOCK, rows),
        out_shape=(
            jax.ShapeDtypeStruct((span, LANES), jnp.float32),
            jax.ShapeDtypeStruct((span // TILE, TILE), jnp.int32),
        ),
        in_specs=[vmem],
        out_specs=(vmem, vmem),
        cost_estimate=pl.CostEstimate(
            flops=4 * span * LANES * span, bytes_accessed=2 << 20, transcendentals=span * span * 4
        ),
    )(qkv)
    mixed = pl.pallas_call(
        memory_kernel,
        out_shape=jax.ShapeDtypeStruct((span, LANES), jnp.bfloat16),
        in_specs=[smem, smem, vmem, vmem] + [hbm] * len(chunks),
        out_specs=vmem,
        scratch_shapes=[
            pltpu.VMEM((SIDE * SIDE * rows, 2 * HEAD_DIM), jnp.bfloat16),
            pltpu.SemaphoreType.DMA((len(chunks),)),
        ],
        cost_estimate=pl.CostEstimate(
            flops=4 * span * LANES * TOPB * BLOCK,
            bytes_accessed=7 << 20,
            transcendentals=span * GROUPS * TOPB * BLOCK,
        ),
    )(starts, gate_bias, qkv, local_out, *chunks)
    back = lax.all_to_all(
        mixed.reshape(members, tokens, LANES), "ctx", split_axis=0, concat_axis=0, tiled=True
    )
    return jnp.transpose(back, (1, 0, 2)).reshape(tokens, HEADS * HEAD_DIM)


def solution(mesh):
    return jax.shard_map(
        body,
        mesh=mesh,
        in_specs=(
            P(("mem", "ctx"), None),
            P(("mem", "ctx"), None),
            P(("mem", "ctx"), None),
            P("mem", None),
            P("mem", None),
            P(("mem", "ctx"), None),
            P(),
        ),
        out_specs=P(("mem", "ctx"), None),
        check_vma=False,
    )
```

```python
import functools

import jax
import jax.numpy as jnp
from jax import lax
from jax.experimental import pallas as pl
from jax.experimental.pallas import tpu as pltpu
from jax.sharding import PartitionSpec as P

HEADS = 32
KV_HEADS = 8
GROUPS = HEADS // KV_HEADS
HEAD_DIM = 128
BLOCK = 32
TOPB = 16
QBLOCK = 16
LANES = GROUPS * HEAD_DIM
EXP2_SCALE = HEAD_DIM ** (-0.5) * 1.4426950408889634
NEG = -1e30
TILE = 128
TOGETHER = 32


def product(left, right, contract_right):
    return lax.dot_general(
        left, right, (((1,), (contract_right,)), ((), ())), preferred_element_type=jnp.float32
    )


def softmax_parts(scores):
    top = jnp.max(scores, axis=-1, keepdims=True)
    weights = jnp.exp2((scores - top) * EXP2_SCALE)
    return weights, jnp.sum(weights, axis=-1, keepdims=True)


def heads_to_rows(rows):
    return jnp.concatenate(
        [rows[:, h * HEAD_DIM : (h + 1) * HEAD_DIM] for h in range(GROUPS)], axis=0
    )


def pack_kernel(
    ids_ref, queries_ref, keys_ref, values_ref, mem_keys_ref, mem_values_ref, out_ref, own_ref, id_ref
):
    for block in range(ids_ref.shape[0]):
        for j in range(TOPB):
            value = ids_ref[block, j].astype(jnp.float32)
            id_ref[block * TOPB + j : block * TOPB + j + 1, :] = jnp.full(
                (1, HEAD_DIM), value, jnp.float32
            )
    id_lanes = id_ref[...].astype(jnp.bfloat16)
    for head in range(KV_HEADS):
        here = slice(head * HEAD_DIM, (head + 1) * HEAD_DIM)
        out_ref[head, :, :LANES] = queries_ref[:, head * LANES : (head + 1) * LANES]
        out_ref[head, :, LANES : LANES + HEAD_DIM] = keys_ref[:, here]
        out_ref[head, :, LANES + HEAD_DIM : LANES + 2 * HEAD_DIM] = values_ref[:, here]
        out_ref[head, :, LANES + 2 * HEAD_DIM :] = id_lanes
    start = pl.multiple_of(lax.axis_index("ctx") * HEAD_DIM, HEAD_DIM)
    keys = mem_keys_ref[:, pl.ds(start, HEAD_DIM)]
    values = mem_values_ref[:, pl.ds(start, HEAD_DIM)]
    for place in range(own_ref.shape[0]):
        own_ref[place, :, :HEAD_DIM] = keys
        own_ref[place, :, HEAD_DIM:] = values


def block_rows(ids, held, rows):
    holder, slot = ids // held, ids % held
    z, y = holder // SIDE, holder % SIDE
    mem = lax.axis_index("mem")
    own_z, own_y = mem // SIDE, mem % SIDE
    first = lax.axis_index("ctx") % 2 == 0
    back = (jnp.where(first, own_y - y, own_z - z) + SIDE) % SIDE
    inner = jnp.where(first, z, y)
    return (back * SIDE + inner) * rows + slot * BLOCK


def local_kernel(held, rows, bias_ref, qkv_ref, out_ref, starts_ref, gates_ref):
    head = lax.axis_index("ctx")
    for h in range(GROUPS):
        bias = jnp.full((1, HEAD_DIM), bias_ref[head * GROUPS + h], jnp.float32)
        gates_ref[h : h + 1, :] = jax.nn.sigmoid(bias)
    span = qkv_ref.shape[0]
    diagonal = lax.broadcasted_iota(jnp.int32, (TILE, HEAD_DIM), 0) == lax.broadcasted_iota(
        jnp.int32, (TILE, HEAD_DIM), 1
    )
    for tile in range(span // TILE):
        ids = qkv_ref[tile * TILE : (tile + 1) * TILE, LANES + 2 * HEAD_DIM :].astype(jnp.float32)
        ids = jnp.sum(jnp.where(diagonal, ids, 0.0), axis=0, keepdims=True).astype(jnp.int32)
        starts_ref[tile : tile + 1, :] = block_rows(ids, held, rows)
    for tile in range(span // TILE):
        lo, hi = tile * TILE, (tile + 1) * TILE
        query = heads_to_rows(qkv_ref[lo:hi, :LANES])
        keys = qkv_ref[:hi, LANES : LANES + HEAD_DIM]
        values = qkv_ref[:hi, LANES + HEAD_DIM : LANES + 2 * HEAD_DIM]
        scores = product(query, keys, 1)
        row = lax.broadcasted_iota(jnp.int32, scores.shape, 0) % TILE + lo
        col = lax.broadcasted_iota(jnp.int32, scores.shape, 1)
        scores = jnp.where(col <= row, scores, NEG)
        weights, total = softmax_parts(scores)
        summed = product(weights.astype(jnp.bfloat16), values, 0) / total
        for h in range(GROUPS):
            out_ref[lo:hi, h * HEAD_DIM : (h + 1) * HEAD_DIM] = summed[
                h * TILE : (h + 1) * TILE
            ]


def picked(store_ref, rows, lanes):
    return jnp.concatenate([store_ref[pl.ds(row, BLOCK), lanes] for row in rows], axis=0)


def memory_kernel(places, starts_ref, gates_ref, qkv_ref, local_ref, *refs):
    chunks, (out_ref, store_ref, sems) = refs[:-3], refs[-3:]
    whole = store_ref.shape[0] // SIDE
    copies = []
    for chunk, backs in zip(chunks, places):
        rows = chunk.shape[0] // len(backs)
        for k, back in enumerate(backs):
            copies.append(
                pltpu.make_async_copy(
                    chunk.at[pl.ds(k * rows, rows)],
                    store_ref.at[pl.ds(int(back * whole), rows)],
                    sems.at[len(copies)],
                )
            )
            copies[-1].start()
    gates = [gates_ref[h : h + 1, :] for h in range(GROUPS)]
    query_blocks = qkv_ref.shape[0] // QBLOCK
    for copy in copies:
        copy.wait()

    for first in range(0, query_blocks, TOGETHER):
        indices = range(first, first + TOGETHER)
        places = [index * QBLOCK for index in indices]
        starts = [
            [pl.multiple_of(starts_ref[divmod(index * TOPB + j, TILE)], BLOCK) for j in range(TOPB)] for index in indices
        ]
        scores = []
        for lo, rows in zip(places, starts):
            query = heads_to_rows(qkv_ref[pl.ds(lo, QBLOCK), :LANES])
            scores.append(product(query, picked(store_ref, rows, slice(0, HEAD_DIM)), 1))
        tops = [jnp.max(score, axis=-1, keepdims=True) for score in scores]
        weights = [jnp.exp2((score - top) * EXP2_SCALE) for score, top in zip(scores, tops)]
        totals = [jnp.sum(weight, axis=-1, keepdims=True) for weight in weights]
        summed = [
            product(
                weight.astype(jnp.bfloat16),
                picked(store_ref, rows, slice(HEAD_DIM, 2 * HEAD_DIM)),
                0,
            )
            for weight, rows in zip(weights, starts)
        ]
        for lo, total, value in zip(places, totals, summed):
            for h in range(GROUPS):
                lanes = slice(h * HEAD_DIM, (h + 1) * HEAD_DIM)
                rows = slice(h * QBLOCK, (h + 1) * QBLOCK)
                memory_out = value[rows] * (gates[h] / total[rows])
                mixed = memory_out + (1.0 - gates[h]) * local_ref[pl.ds(lo, QBLOCK), lanes]
                out_ref[pl.ds(lo, QBLOCK), lanes] = mixed.astype(jnp.bfloat16)


BOTH = ("mem", "ctx")
SIDE = 8
CTX = 8


def device(z, y, ctx):
    return (z * SIDE + y) * CTX + ctx


def ring_of(ctx):
    return ctx % 2


def first_groups():
    groups = []
    for ctx in range(CTX):
        for other in range(SIDE):
            if ring_of(ctx) == 0:
                groups.append([device(z, other, ctx) for z in range(SIDE)])
            else:
                groups.append([device(other, y, ctx) for y in range(SIDE)])
    return groups


def shifted(value, step):
    pairs = []
    for z in range(SIDE):
        for y in range(SIDE):
            for ctx in range(CTX):
                if ring_of(ctx) == 0:
                    target = device(z, (y + step) % SIDE, ctx)
                else:
                    target = device((z + step) % SIDE, y, ctx)
                pairs.append((device(z, y, ctx), target))
    return lax.ppermute(value, BOTH, pairs)


def join_kernel(chunk_ref, ahead_ref, behind_ref, *refs):
    (ahead_pair, behind_pair, ahead_half, behind_half), sems = refs[:4], refs[4]
    rows = chunk_ref.shape[0]
    half = rows // 2
    moves = [
        (chunk_ref, ahead_pair.at[pl.ds(0, rows)]),
        (ahead_ref, ahead_pair.at[pl.ds(rows, rows)]),
        (chunk_ref, behind_pair.at[pl.ds(0, rows)]),
        (behind_ref, behind_pair.at[pl.ds(rows, rows)]),
        (ahead_ref.at[pl.ds(0, half)], ahead_half),
        (behind_ref.at[pl.ds(half, half)], behind_half),
    ]
    copies = [
        pltpu.make_async_copy(source, target, sems.at[i])
        for i, (source, target) in enumerate(moves)
    ]
    for copy in copies:
        copy.start()
    for copy in copies:
        copy.wait()


def gathered(chunk, qkv):
    rows, width = chunk.shape
    ahead2, behind2 = shifted(chunk, 2), shifted(chunk, -2)
    hbm = pl.BlockSpec(memory_space=pl.ANY)
    joined = pl.pallas_call(
        join_kernel,
        out_shape=[
            jax.ShapeDtypeStruct((count, width), chunk.dtype)
            for count in (2 * rows, 2 * rows, rows // 2, rows // 2)
        ],
        in_specs=[hbm] * 3,
        out_specs=[pl.BlockSpec(memory_space=pltpu.HBM)] * 4,
        scratch_shapes=[pltpu.SemaphoreType.DMA((6,))],
        compiler_params=pltpu.CompilerParams(vmem_limit_bytes=1 << 20),
        cost_estimate=pl.CostEstimate(flops=0, bytes_accessed=5 << 20, transcendentals=0),
    )(chunk, ahead2, behind2)
    ahead13, behind13 = shifted(joined[0], 1), shifted(joined[1], -1)
    ahead_half, behind_half, qkv = lax.optimization_barrier((joined[2], joined[3], qkv))
    ahead4, behind4 = shifted(ahead_half, 2), shifted(behind_half, -2)
    return qkv, [
        (chunk, (0,)),
        (ahead13, (1, 3)),
        (ahead2, (2,)),
        (ahead4, (4,)),
        (behind4, (4.5,)),
        (behind13, (7, 5)),
        (behind2, (6,)),
    ]


def body(queries, local_keys, local_values, mem_keys, mem_values, block_ids, gate_bias):
    tokens = queries.shape[0]
    members = lax.axis_size("ctx")
    span = tokens * members
    rows = mem_keys.shape[0]
    vmem = pl.BlockSpec(memory_space=pltpu.VMEM)
    smem = pl.BlockSpec(memory_space=pltpu.SMEM)
    hbm = pl.BlockSpec(memory_space=pl.ANY)
    packed, spread = pl.pallas_call(
        pack_kernel,
        out_shape=(
            jax.ShapeDtypeStruct((members, tokens, LANES + 3 * HEAD_DIM), jnp.bfloat16),
            jax.ShapeDtypeStruct((SIDE, rows, 2 * HEAD_DIM), jnp.bfloat16),
        ),
        in_specs=[smem] + [vmem] * 5,
        out_specs=(vmem, vmem),
        scratch_shapes=[pltpu.VMEM((tokens, HEAD_DIM), jnp.float32)],
        cost_estimate=pl.CostEstimate(flops=0, bytes_accessed=4 << 20, transcendentals=0),
    )(block_ids, queries, local_keys, local_values, mem_keys, mem_values)
    qkv = lax.all_to_all(packed, "ctx", split_axis=0, concat_axis=0, tiled=True)
    qkv = qkv.reshape(span, LANES + 3 * HEAD_DIM)
    chunk = lax.all_to_all(
        spread, BOTH, split_axis=0, concat_axis=0, tiled=True, axis_index_groups=first_groups()
    ).reshape(SIDE * rows, 2 * HEAD_DIM)
    qkv, pieces = gathered(chunk, qkv)
    chunks, places = [piece for piece, _ in pieces], [backs for _, backs in pieces]
    local_out, starts, gates = pl.pallas_call(
        functools.partial(local_kernel, rows // BLOCK, rows),
        out_shape=(
            jax.ShapeDtypeStruct((span, LANES), jnp.float32),
            jax.ShapeDtypeStruct((span // TILE, TILE), jnp.int32),
            jax.ShapeDtypeStruct((GROUPS, HEAD_DIM), jnp.float32),
        ),
        in_specs=[smem, vmem],
        out_specs=(vmem, vmem, vmem),
        compiler_params=pltpu.CompilerParams(vmem_limit_bytes=12 << 20),
        cost_estimate=pl.CostEstimate(
            flops=4 * span * LANES * span, bytes_accessed=2 << 20, transcendentals=span * span * 4
        ),
    )(gate_bias, qkv)
    mixed = pl.pallas_call(
        functools.partial(memory_kernel, places),
        out_shape=jax.ShapeDtypeStruct((span, LANES), jnp.bfloat16),
        in_specs=[smem, vmem, vmem, vmem] + [hbm] * len(chunks),
        out_specs=vmem,
        scratch_shapes=[
            pltpu.VMEM((SIDE * SIDE * rows, 2 * HEAD_DIM), jnp.bfloat16),
            pltpu.SemaphoreType.DMA((sum(map(len, places)),)),
        ],
        compiler_params=pltpu.CompilerParams(vmem_limit_bytes=32 << 20),
        cost_estimate=pl.CostEstimate(
            flops=4 * span * LANES * TOPB * BLOCK,
            bytes_accessed=7 << 20,
            transcendentals=span * GROUPS * TOPB * BLOCK,
        ),
    )(starts, gates, qkv, local_out, *chunks)
    back = lax.all_to_all(
        mixed.reshape(members, tokens, LANES), "ctx", split_axis=0, concat_axis=0, tiled=True
    )
    return jnp.transpose(back, (1, 0, 2)).reshape(tokens, HEADS * HEAD_DIM)


def solution(mesh):
    return jax.shard_map(
        body,
        mesh=mesh,
        in_specs=(
            P(("mem", "ctx"), None),
            P(("mem", "ctx"), None),
            P(("mem", "ctx"), None),
            P("mem", None),
            P("mem", None),
            P(("mem", "ctx"), None),
            P(),
        ),
        out_specs=P(("mem", "ctx"), None),
        check_vma=False,
    )
```

```python
import functools

import jax
import jax.numpy as jnp
from jax import lax
from jax.experimental import pallas as pl
from jax.experimental.pallas import tpu as pltpu
from jax.sharding import PartitionSpec as P

HEADS = 32
KV_HEADS = 8
GROUPS = HEADS // KV_HEADS
HEAD_DIM = 128
BLOCK = 32
TOPB = 16
QBLOCK = 16
LANES = GROUPS * HEAD_DIM
EXP2_SCALE = HEAD_DIM ** (-0.5) * 1.4426950408889634
NEG = -1e30
TILE = 128
TOGETHER = 32


def product(left, right, contract_right):
    return lax.dot_general(
        left, right, (((1,), (contract_right,)), ((), ())), preferred_element_type=jnp.float32
    )


def softmax_parts(scores):
    top = jnp.max(scores, axis=-1, keepdims=True)
    weights = jnp.exp2((scores - top) * EXP2_SCALE)
    return weights, jnp.sum(weights, axis=-1, keepdims=True)


def heads_to_rows(rows):
    return jnp.concatenate(
        [rows[:, h * HEAD_DIM : (h + 1) * HEAD_DIM] for h in range(GROUPS)], axis=0
    )


def pack_kernel(
    ids_ref, queries_ref, keys_ref, values_ref, mem_keys_ref, mem_values_ref, out_ref, own_ref, id_ref
):
    for block in range(ids_ref.shape[0]):
        for j in range(TOPB):
            value = ids_ref[block, j].astype(jnp.float32)
            id_ref[block * TOPB + j : block * TOPB + j + 1, :] = jnp.full(
                (1, HEAD_DIM), value, jnp.float32
            )
    id_lanes = id_ref[...].astype(jnp.bfloat16)
    for head in range(KV_HEADS):
        here = slice(head * HEAD_DIM, (head + 1) * HEAD_DIM)
        out_ref[head, :, :LANES] = queries_ref[:, head * LANES : (head + 1) * LANES]
        out_ref[head, :, LANES : LANES + HEAD_DIM] = keys_ref[:, here]
        out_ref[head, :, LANES + HEAD_DIM : LANES + 2 * HEAD_DIM] = values_ref[:, here]
        out_ref[head, :, LANES + 2 * HEAD_DIM :] = id_lanes
    start = pl.multiple_of(lax.axis_index("ctx") * HEAD_DIM, HEAD_DIM)
    keys = mem_keys_ref[:, pl.ds(start, HEAD_DIM)]
    values = mem_values_ref[:, pl.ds(start, HEAD_DIM)]
    for place in range(own_ref.shape[0]):
        own_ref[place, :, :HEAD_DIM] = keys
        own_ref[place, :, HEAD_DIM:] = values


def block_rows(ids, held, rows):
    holder, slot = ids // held, ids % held
    z, y = holder // SIDE, holder % SIDE
    mem = lax.axis_index("mem")
    own_z, own_y = mem // SIDE, mem % SIDE
    first = lax.axis_index("ctx") % 2 == 0
    back = (jnp.where(first, own_y - y, own_z - z) + SIDE) % SIDE
    inner = jnp.where(first, z, y)
    return (back * SIDE + inner) * rows + slot * BLOCK


def local_kernel(held, rows, bias_ref, qkv_ref, out_ref, starts_ref, gates_ref):
    head = lax.axis_index("ctx")
    for h in range(GROUPS):
        bias = jnp.full((1, HEAD_DIM), bias_ref[head * GROUPS + h], jnp.float32)
        gates_ref[h : h + 1, :] = jax.nn.sigmoid(bias)
    span = qkv_ref.shape[0]
    diagonal = lax.broadcasted_iota(jnp.int32, (TILE, HEAD_DIM), 0) == lax.broadcasted_iota(
        jnp.int32, (TILE, HEAD_DIM), 1
    )
    for tile in range(span // TILE):
        ids = qkv_ref[tile * TILE : (tile + 1) * TILE, LANES + 2 * HEAD_DIM :].astype(jnp.float32)
        ids = jnp.sum(jnp.where(diagonal, ids, 0.0), axis=0, keepdims=True).astype(jnp.int32)
        starts_ref[tile : tile + 1, :] = block_rows(ids, held, rows)
    for tile in range(span // TILE):
        lo, hi = tile * TILE, (tile + 1) * TILE
        query = heads_to_rows(qkv_ref[lo:hi, :LANES])
        keys = qkv_ref[:hi, LANES : LANES + HEAD_DIM]
        values = qkv_ref[:hi, LANES + HEAD_DIM : LANES + 2 * HEAD_DIM]
        scores = product(query, keys, 1)
        row = lax.broadcasted_iota(jnp.int32, scores.shape, 0) % TILE + lo
        col = lax.broadcasted_iota(jnp.int32, scores.shape, 1)
        scores = jnp.where(col <= row, scores, NEG)
        weights, total = softmax_parts(scores)
        summed = product(weights.astype(jnp.bfloat16), values, 0) / total
        for h in range(GROUPS):
            out_ref[lo:hi, h * HEAD_DIM : (h + 1) * HEAD_DIM] = summed[
                h * TILE : (h + 1) * TILE
            ]


def picked(store_ref, rows, lanes):
    return jnp.concatenate([store_ref[pl.ds(row, BLOCK), lanes] for row in rows], axis=0)


def memory_kernel(starts_ref, gates_ref, qkv_ref, local_ref, *refs):
    chunks, (out_ref, store_ref, sems) = refs[:-3], refs[-3:]
    copies, row = [], 0
    for i, chunk in enumerate(chunks):
        rows = chunk.shape[0]
        copies.append(
            pltpu.make_async_copy(chunk, store_ref.at[pl.ds(row, rows)], sems.at[i])
        )
        copies[-1].start()
        row += rows
    gates = [gates_ref[h : h + 1, :] for h in range(GROUPS)]
    query_blocks = qkv_ref.shape[0] // QBLOCK
    for copy in copies:
        copy.wait()

    for first in range(0, query_blocks, TOGETHER):
        indices = range(first, first + TOGETHER)
        places = [index * QBLOCK for index in indices]
        starts = [
            [pl.multiple_of(starts_ref[divmod(index * TOPB + j, TILE)], BLOCK) for j in range(TOPB)] for index in indices
        ]
        scores = []
        for lo, rows in zip(places, starts):
            query = heads_to_rows(qkv_ref[pl.ds(lo, QBLOCK), :LANES])
            scores.append(product(query, picked(store_ref, rows, slice(0, HEAD_DIM)), 1))
        tops = [jnp.max(score, axis=-1, keepdims=True) for score in scores]
        weights = [jnp.exp2((score - top) * EXP2_SCALE) for score, top in zip(scores, tops)]
        totals = [jnp.sum(weight, axis=-1, keepdims=True) for weight in weights]
        summed = [
            product(
                weight.astype(jnp.bfloat16),
                picked(store_ref, rows, slice(HEAD_DIM, 2 * HEAD_DIM)),
                0,
            )
            for weight, rows in zip(weights, starts)
        ]
        for lo, total, value in zip(places, totals, summed):
            for h in range(GROUPS):
                lanes = slice(h * HEAD_DIM, (h + 1) * HEAD_DIM)
                rows = slice(h * QBLOCK, (h + 1) * QBLOCK)
                memory_out = value[rows] * (gates[h] / total[rows])
                mixed = memory_out + (1.0 - gates[h]) * local_ref[pl.ds(lo, QBLOCK), lanes]
                out_ref[pl.ds(lo, QBLOCK), lanes] = mixed.astype(jnp.bfloat16)


BOTH = ("mem", "ctx")
SIDE = 8
CTX = 8


def device(z, y, ctx):
    return (z * SIDE + y) * CTX + ctx


def ring_of(ctx):
    return ctx % 2


def first_groups():
    groups = []
    for ctx in range(CTX):
        for other in range(SIDE):
            if ring_of(ctx) == 0:
                groups.append([device(z, other, ctx) for z in range(SIDE)])
            else:
                groups.append([device(other, y, ctx) for y in range(SIDE)])
    return groups


def shifted(value, step):
    pairs = []
    for z in range(SIDE):
        for y in range(SIDE):
            for ctx in range(CTX):
                if ring_of(ctx) == 0:
                    target = device(z, (y + step) % SIDE, ctx)
                else:
                    target = device((z + step) % SIDE, y, ctx)
                pairs.append((device(z, y, ctx), target))
    return lax.ppermute(value, BOTH, pairs)


def gathered(chunk):
    ahead2, behind2 = shifted(chunk, 2), shifted(chunk, -2)
    ahead1, behind1 = shifted(chunk, 1), shifted(chunk, -1)
    ahead3, behind3 = shifted(ahead2, 1), shifted(behind2, -1)
    half = chunk.shape[0] // 2
    ahead4, behind4 = shifted(ahead2[:half], 2), shifted(behind2[half:], -2)
    return [chunk, ahead1, ahead2, ahead3, ahead4, behind4, behind3, behind2, behind1]


def body(queries, local_keys, local_values, mem_keys, mem_values, block_ids, gate_bias):
    tokens = queries.shape[0]
    members = lax.axis_size("ctx")
    span = tokens * members
    rows = mem_keys.shape[0]
    vmem = pl.BlockSpec(memory_space=pltpu.VMEM)
    smem = pl.BlockSpec(memory_space=pltpu.SMEM)
    hbm = pl.BlockSpec(memory_space=pl.ANY)
    packed, spread = pl.pallas_call(
        pack_kernel,
        out_shape=(
            jax.ShapeDtypeStruct((members, tokens, LANES + 3 * HEAD_DIM), jnp.bfloat16),
            jax.ShapeDtypeStruct((SIDE, rows, 2 * HEAD_DIM), jnp.bfloat16),
        ),
        in_specs=[smem] + [vmem] * 5,
        out_specs=(vmem, vmem),
        scratch_shapes=[pltpu.VMEM((tokens, HEAD_DIM), jnp.float32)],
        cost_estimate=pl.CostEstimate(flops=0, bytes_accessed=4 << 20, transcendentals=0),
    )(block_ids, queries, local_keys, local_values, mem_keys, mem_values)
    qkv = lax.all_to_all(packed, "ctx", split_axis=0, concat_axis=0, tiled=True)
    qkv = qkv.reshape(span, LANES + 3 * HEAD_DIM)
    chunk = lax.all_to_all(
        spread, BOTH, split_axis=0, concat_axis=0, tiled=True, axis_index_groups=first_groups()
    ).reshape(SIDE * rows, 2 * HEAD_DIM)
    chunks = gathered(chunk)
    local_out, starts, gates = pl.pallas_call(
        functools.partial(local_kernel, rows // BLOCK, rows),
        out_shape=(
            jax.ShapeDtypeStruct((span, LANES), jnp.float32),
            jax.ShapeDtypeStruct((span // TILE, TILE), jnp.int32),
            jax.ShapeDtypeStruct((GROUPS, HEAD_DIM), jnp.float32),
        ),
        in_specs=[smem, vmem],
        out_specs=(vmem, vmem, vmem),
        compiler_params=pltpu.CompilerParams(vmem_limit_bytes=12 << 20),
        cost_estimate=pl.CostEstimate(
            flops=4 * span * LANES * span, bytes_accessed=2 << 20, transcendentals=span * span * 4
        ),
    )(gate_bias, qkv)
    mixed = pl.pallas_call(
        memory_kernel,
        out_shape=jax.ShapeDtypeStruct((span, LANES), jnp.bfloat16),
        in_specs=[smem, vmem, vmem, vmem] + [hbm] * len(chunks),
        out_specs=vmem,
        scratch_shapes=[
            pltpu.VMEM((SIDE * SIDE * rows, 2 * HEAD_DIM), jnp.bfloat16),
            pltpu.SemaphoreType.DMA((len(chunks),)),
        ],
        compiler_params=pltpu.CompilerParams(vmem_limit_bytes=32 << 20),
        cost_estimate=pl.CostEstimate(
            flops=4 * span * LANES * TOPB * BLOCK,
            bytes_accessed=7 << 20,
            transcendentals=span * GROUPS * TOPB * BLOCK,
        ),
    )(starts, gates, qkv, local_out, *chunks)
    back = lax.all_to_all(
        mixed.reshape(members, tokens, LANES), "ctx", split_axis=0, concat_axis=0, tiled=True
    )
    return jnp.transpose(back, (1, 0, 2)).reshape(tokens, HEADS * HEAD_DIM)


def solution(mesh):
    return jax.shard_map(
        body,
        mesh=mesh,
        in_specs=(
            P(("mem", "ctx"), None),
            P(("mem", "ctx"), None),
            P(("mem", "ctx"), None),
            P("mem", None),
            P("mem", None),
            P(("mem", "ctx"), None),
            P(),
        ),
        out_specs=P(("mem", "ctx"), None),
        check_vma=False,
    )
```

```python
import functools

import jax
import jax.numpy as jnp
from jax import lax
from jax.experimental import pallas as pl
from jax.experimental.pallas import tpu as pltpu
from jax.sharding import PartitionSpec as P

HEADS = 32
KV_HEADS = 8
GROUPS = HEADS // KV_HEADS
HEAD_DIM = 128
BLOCK = 32
TOPB = 16
QBLOCK = 16
LANES = GROUPS * HEAD_DIM
EXP2_SCALE = HEAD_DIM ** (-0.5) * 1.4426950408889634
NEG = -1e30
TILE = 128
TOGETHER = 32


def product(left, right, contract_right):
    return lax.dot_general(
        left, right, (((1,), (contract_right,)), ((), ())), preferred_element_type=jnp.float32
    )


def softmax_parts(scores):
    top = jnp.max(scores, axis=-1, keepdims=True)
    weights = jnp.exp2((scores - top) * EXP2_SCALE)
    return weights, jnp.sum(weights, axis=-1, keepdims=True)


def heads_to_rows(rows):
    return jnp.concatenate(
        [rows[:, h * HEAD_DIM : (h + 1) * HEAD_DIM] for h in range(GROUPS)], axis=0
    )


def pack_kernel(
    ids_ref, queries_ref, keys_ref, values_ref, mem_keys_ref, mem_values_ref, out_ref, own_ref, id_ref
):
    for block in range(ids_ref.shape[0]):
        for j in range(TOPB):
            value = ids_ref[block, j].astype(jnp.float32)
            id_ref[block * TOPB + j : block * TOPB + j + 1, :] = jnp.full(
                (1, HEAD_DIM), value, jnp.float32
            )
    id_lanes = id_ref[...].astype(jnp.bfloat16)
    for head in range(KV_HEADS):
        here = slice(head * HEAD_DIM, (head + 1) * HEAD_DIM)
        out_ref[head, :, :LANES] = queries_ref[:, head * LANES : (head + 1) * LANES]
        out_ref[head, :, LANES : LANES + HEAD_DIM] = keys_ref[:, here]
        out_ref[head, :, LANES + HEAD_DIM : LANES + 2 * HEAD_DIM] = values_ref[:, here]
        out_ref[head, :, LANES + 2 * HEAD_DIM :] = id_lanes
    start = pl.multiple_of(lax.axis_index("ctx") * HEAD_DIM, HEAD_DIM)
    keys = mem_keys_ref[:, pl.ds(start, HEAD_DIM)]
    values = mem_values_ref[:, pl.ds(start, HEAD_DIM)]
    for place in range(own_ref.shape[0]):
        own_ref[place, :, :HEAD_DIM] = keys
        own_ref[place, :, HEAD_DIM:] = values


def block_rows(ids, held, rows):
    holder, slot = ids // held, ids % held
    z, y = holder // SIDE, holder % SIDE
    mem = lax.axis_index("mem")
    own_z, own_y = mem // SIDE, mem % SIDE
    first = lax.axis_index("ctx") % 2 == 0
    back = (jnp.where(first, own_y - y, own_z - z) + SIDE) % SIDE
    inner = jnp.where(first, z, y)
    return (back * SIDE + inner) * rows + slot * BLOCK


def local_kernel(held, rows, bias_ref, qkv_ref, out_ref, starts_ref, gates_ref):
    head = lax.axis_index("ctx")
    for h in range(GROUPS):
        bias = jnp.full((1, HEAD_DIM), bias_ref[head * GROUPS + h], jnp.float32)
        gates_ref[h : h + 1, :] = jax.nn.sigmoid(bias)
    span = qkv_ref.shape[0]
    diagonal = lax.broadcasted_iota(jnp.int32, (TILE, HEAD_DIM), 0) == lax.broadcasted_iota(
        jnp.int32, (TILE, HEAD_DIM), 1
    )
    for tile in range(span // TILE):
        ids = qkv_ref[tile * TILE : (tile + 1) * TILE, LANES + 2 * HEAD_DIM :].astype(jnp.float32)
        ids = jnp.sum(jnp.where(diagonal, ids, 0.0), axis=0, keepdims=True).astype(jnp.int32)
        starts_ref[tile : tile + 1, :] = block_rows(ids, held, rows)
    for tile in range(span // TILE):
        lo, hi = tile * TILE, (tile + 1) * TILE
        query = heads_to_rows(qkv_ref[lo:hi, :LANES])
        keys = qkv_ref[:hi, LANES : LANES + HEAD_DIM]
        values = qkv_ref[:hi, LANES + HEAD_DIM : LANES + 2 * HEAD_DIM]
        scores = product(query, keys, 1)
        row = lax.broadcasted_iota(jnp.int32, scores.shape, 0) % TILE + lo
        col = lax.broadcasted_iota(jnp.int32, scores.shape, 1)
        scores = jnp.where(col <= row, scores, NEG)
        weights, total = softmax_parts(scores)
        summed = product(weights.astype(jnp.bfloat16), values, 0) / total
        for h in range(GROUPS):
            out_ref[lo:hi, h * HEAD_DIM : (h + 1) * HEAD_DIM] = summed[
                h * TILE : (h + 1) * TILE
            ]


def picked(store_ref, rows, lanes):
    return jnp.concatenate([store_ref[pl.ds(row, BLOCK), lanes] for row in rows], axis=0)


def memory_kernel(starts_ref, gates_ref, qkv_ref, local_ref, *refs):
    chunks, (out_ref, store_ref, sems) = refs[:-3], refs[-3:]
    copies, row = [], 0
    for i, chunk in enumerate(chunks):
        rows = chunk.shape[0]
        copies.append(
            pltpu.make_async_copy(chunk, store_ref.at[pl.ds(row, rows)], sems.at[i])
        )
        copies[-1].start()
        row += rows
    gates = [gates_ref[h : h + 1, :] for h in range(GROUPS)]
    query_blocks = qkv_ref.shape[0] // QBLOCK
    for copy in copies:
        copy.wait()

    for first in range(0, query_blocks, TOGETHER):
        indices = range(first, first + TOGETHER)
        places = [index * QBLOCK for index in indices]
        starts = [
            [pl.multiple_of(starts_ref[divmod(index * TOPB + j, TILE)], BLOCK) for j in range(TOPB)] for index in indices
        ]
        scores = []
        for lo, rows in zip(places, starts):
            query = heads_to_rows(qkv_ref[pl.ds(lo, QBLOCK), :LANES])
            scores.append(product(query, picked(store_ref, rows, slice(0, HEAD_DIM)), 1))
        tops = [jnp.max(score, axis=-1, keepdims=True) for score in scores]
        weights = [jnp.exp2((score - top) * EXP2_SCALE) for score, top in zip(scores, tops)]
        totals = [jnp.sum(weight, axis=-1, keepdims=True) for weight in weights]
        summed = [
            product(
                weight.astype(jnp.bfloat16),
                picked(store_ref, rows, slice(HEAD_DIM, 2 * HEAD_DIM)),
                0,
            )
            for weight, rows in zip(weights, starts)
        ]
        for lo, total, value in zip(places, totals, summed):
            for h in range(GROUPS):
                lanes = slice(h * HEAD_DIM, (h + 1) * HEAD_DIM)
                rows = slice(h * QBLOCK, (h + 1) * QBLOCK)
                memory_out = value[rows] * (gates[h] / total[rows])
                mixed = memory_out + (1.0 - gates[h]) * local_ref[pl.ds(lo, QBLOCK), lanes]
                out_ref[pl.ds(lo, QBLOCK), lanes] = mixed.astype(jnp.bfloat16)


BOTH = ("mem", "ctx")
SIDE = 8
CTX = 8


def device(z, y, ctx):
    return (z * SIDE + y) * CTX + ctx


def ring_of(ctx):
    return ctx % 2


def first_groups():
    groups = []
    for ctx in range(CTX):
        for other in range(SIDE):
            if ring_of(ctx) == 0:
                groups.append([device(z, other, ctx) for z in range(SIDE)])
            else:
                groups.append([device(other, y, ctx) for y in range(SIDE)])
    return groups


def moved(value, target):
    pairs = []
    for z in range(SIDE):
        for y in range(SIDE):
            for ctx in range(CTX):
                if ring_of(ctx) == 0:
                    to = device(z, target(y) % SIDE, ctx)
                else:
                    to = device(target(z) % SIDE, y, ctx)
                pairs.append((device(z, y, ctx), to))
    return lax.ppermute(value, BOTH, pairs)


def shifted(value, step):
    return moved(value, lambda place: place + step)


def ring_place():
    mem = lax.axis_index("mem")
    return jnp.where(lax.axis_index("ctx") % 2 == 0, mem % SIDE, mem // SIDE)


def gathered(chunk):
    ahead2, behind2 = shifted(chunk, 2), shifted(chunk, -2)
    ahead1, behind1 = shifted(chunk, 1), shifted(chunk, -1)
    ahead3, behind3 = shifted(ahead2, 1), shifted(behind2, -1)
    onward = jnp.where(ring_place() % 2 == 0, ahead2, behind2)
    far = moved(onward, lambda place: place + 2 if place % 2 == 0 else place - 2)
    return [chunk, ahead1, ahead2, ahead3, far, behind3, behind2, behind1]


def body(queries, local_keys, local_values, mem_keys, mem_values, block_ids, gate_bias):
    tokens = queries.shape[0]
    members = lax.axis_size("ctx")
    span = tokens * members
    rows = mem_keys.shape[0]
    vmem = pl.BlockSpec(memory_space=pltpu.VMEM)
    smem = pl.BlockSpec(memory_space=pltpu.SMEM)
    hbm = pl.BlockSpec(memory_space=pl.ANY)
    packed, spread = pl.pallas_call(
        pack_kernel,
        out_shape=(
            jax.ShapeDtypeStruct((members, tokens, LANES + 3 * HEAD_DIM), jnp.bfloat16),
            jax.ShapeDtypeStruct((SIDE, rows, 2 * HEAD_DIM), jnp.bfloat16),
        ),
        in_specs=[smem] + [vmem] * 5,
        out_specs=(vmem, vmem),
        scratch_shapes=[pltpu.VMEM((tokens, HEAD_DIM), jnp.float32)],
        cost_estimate=pl.CostEstimate(flops=0, bytes_accessed=4 << 20, transcendentals=0),
    )(block_ids, queries, local_keys, local_values, mem_keys, mem_values)
    qkv = lax.all_to_all(packed, "ctx", split_axis=0, concat_axis=0, tiled=True)
    qkv = qkv.reshape(span, LANES + 3 * HEAD_DIM)
    chunk = lax.all_to_all(
        spread, BOTH, split_axis=0, concat_axis=0, tiled=True, axis_index_groups=first_groups()
    ).reshape(SIDE * rows, 2 * HEAD_DIM)
    chunks = gathered(chunk)
    local_out, starts, gates = pl.pallas_call(
        functools.partial(local_kernel, rows // BLOCK, rows),
        out_shape=(
            jax.ShapeDtypeStruct((span, LANES), jnp.float32),
            jax.ShapeDtypeStruct((span // TILE, TILE), jnp.int32),
            jax.ShapeDtypeStruct((GROUPS, HEAD_DIM), jnp.float32),
        ),
        in_specs=[smem, vmem],
        out_specs=(vmem, vmem, vmem),
        compiler_params=pltpu.CompilerParams(vmem_limit_bytes=12 << 20),
        cost_estimate=pl.CostEstimate(
            flops=4 * span * LANES * span, bytes_accessed=2 << 20, transcendentals=span * span * 4
        ),
    )(gate_bias, qkv)
    mixed = pl.pallas_call(
        memory_kernel,
        out_shape=jax.ShapeDtypeStruct((span, LANES), jnp.bfloat16),
        in_specs=[smem, vmem, vmem, vmem] + [hbm] * len(chunks),
        out_specs=vmem,
        scratch_shapes=[
            pltpu.VMEM((SIDE * SIDE * rows, 2 * HEAD_DIM), jnp.bfloat16),
            pltpu.SemaphoreType.DMA((len(chunks),)),
        ],
        compiler_params=pltpu.CompilerParams(vmem_limit_bytes=32 << 20),
        cost_estimate=pl.CostEstimate(
            flops=4 * span * LANES * TOPB * BLOCK,
            bytes_accessed=7 << 20,
            transcendentals=span * GROUPS * TOPB * BLOCK,
        ),
    )(starts, gates, qkv, local_out, *chunks)
    back = lax.all_to_all(
        mixed.reshape(members, tokens, LANES), "ctx", split_axis=0, concat_axis=0, tiled=True
    )
    return jnp.transpose(back, (1, 0, 2)).reshape(tokens, HEADS * HEAD_DIM)


def solution(mesh):
    return jax.shard_map(
        body,
        mesh=mesh,
        in_specs=(
            P(("mem", "ctx"), None),
            P(("mem", "ctx"), None),
            P(("mem", "ctx"), None),
            P("mem", None),
            P("mem", None),
            P(("mem", "ctx"), None),
            P(),
        ),
        out_specs=P(("mem", "ctx"), None),
        check_vma=False,
    )
```

```python
import functools

import jax
import jax.numpy as jnp
from jax import lax
from jax.experimental import pallas as pl
from jax.experimental.pallas import tpu as pltpu
from jax.sharding import PartitionSpec as P

HEADS = 32
KV_HEADS = 8
GROUPS = HEADS // KV_HEADS
HEAD_DIM = 128
BLOCK = 32
TOPB = 16
QBLOCK = 16
LANES = GROUPS * HEAD_DIM
EXP2_SCALE = HEAD_DIM ** (-0.5) * 1.4426950408889634
NEG = -1e30
TILE = 128
TOGETHER = 32


def product(left, right, contract_right):
    return lax.dot_general(
        left, right, (((1,), (contract_right,)), ((), ())), preferred_element_type=jnp.float32
    )


def softmax_parts(scores):
    top = jnp.max(scores, axis=-1, keepdims=True)
    weights = jnp.exp2((scores - top) * EXP2_SCALE)
    return weights, jnp.sum(weights, axis=-1, keepdims=True)


def heads_to_rows(rows):
    return jnp.concatenate(
        [rows[:, h * HEAD_DIM : (h + 1) * HEAD_DIM] for h in range(GROUPS)], axis=0
    )


def pack_kernel(
    ids_ref, queries_ref, keys_ref, values_ref, mem_keys_ref, mem_values_ref, out_ref, own_ref, id_ref
):
    for block in range(ids_ref.shape[0]):
        for j in range(TOPB):
            value = ids_ref[block, j].astype(jnp.float32)
            id_ref[block * TOPB + j : block * TOPB + j + 1, :] = jnp.full(
                (1, HEAD_DIM), value, jnp.float32
            )
    id_lanes = id_ref[...].astype(jnp.bfloat16)
    for head in range(KV_HEADS):
        here = slice(head * HEAD_DIM, (head + 1) * HEAD_DIM)
        out_ref[head, :, :LANES] = queries_ref[:, head * LANES : (head + 1) * LANES]
        out_ref[head, :, LANES : LANES + HEAD_DIM] = keys_ref[:, here]
        out_ref[head, :, LANES + HEAD_DIM : LANES + 2 * HEAD_DIM] = values_ref[:, here]
        out_ref[head, :, LANES + 2 * HEAD_DIM :] = id_lanes
    start = pl.multiple_of(lax.axis_index("ctx") * HEAD_DIM, HEAD_DIM)
    keys = mem_keys_ref[:, pl.ds(start, HEAD_DIM)]
    values = mem_values_ref[:, pl.ds(start, HEAD_DIM)]
    for place in range(own_ref.shape[0]):
        own_ref[place, :, :HEAD_DIM] = keys
        own_ref[place, :, HEAD_DIM:] = values


def block_rows(ids, held, rows):
    holder, slot = ids // held, ids % held
    z, y = holder // SIDE, holder % SIDE
    mem = lax.axis_index("mem")
    own_z, own_y = mem // SIDE, mem % SIDE
    first = lax.axis_index("ctx") % 2 == 0
    back = (jnp.where(first, own_y - y, own_z - z) + SIDE) % SIDE
    inner = jnp.where(first, z, y)
    return (back * SIDE + inner) * rows + slot * BLOCK


def local_kernel(held, rows, bias_ref, qkv_ref, out_ref, starts_ref, gates_ref):
    head = lax.axis_index("ctx")
    for h in range(GROUPS):
        bias = jnp.full((1, HEAD_DIM), bias_ref[head * GROUPS + h], jnp.float32)
        gates_ref[h : h + 1, :] = jax.nn.sigmoid(bias)
    span = qkv_ref.shape[0]
    diagonal = lax.broadcasted_iota(jnp.int32, (TILE, HEAD_DIM), 0) == lax.broadcasted_iota(
        jnp.int32, (TILE, HEAD_DIM), 1
    )
    for tile in range(span // TILE):
        ids = qkv_ref[tile * TILE : (tile + 1) * TILE, LANES + 2 * HEAD_DIM :].astype(jnp.float32)
        ids = jnp.sum(jnp.where(diagonal, ids, 0.0), axis=0, keepdims=True).astype(jnp.int32)
        starts_ref[tile : tile + 1, :] = block_rows(ids, held, rows)
    for tile in range(span // TILE):
        lo, hi = tile * TILE, (tile + 1) * TILE
        query = heads_to_rows(qkv_ref[lo:hi, :LANES])
        keys = qkv_ref[:hi, LANES : LANES + HEAD_DIM]
        values = qkv_ref[:hi, LANES + HEAD_DIM : LANES + 2 * HEAD_DIM]
        scores = product(query, keys, 1)
        row = lax.broadcasted_iota(jnp.int32, scores.shape, 0) % TILE + lo
        col = lax.broadcasted_iota(jnp.int32, scores.shape, 1)
        scores = jnp.where(col <= row, scores, NEG)
        weights, total = softmax_parts(scores)
        summed = product(weights.astype(jnp.bfloat16), values, 0) / total
        for h in range(GROUPS):
            out_ref[lo:hi, h * HEAD_DIM : (h + 1) * HEAD_DIM] = summed[
                h * TILE : (h + 1) * TILE
            ]


def picked(store_ref, rows, lanes):
    return jnp.concatenate([store_ref[pl.ds(row, BLOCK), lanes] for row in rows], axis=0)


def memory_kernel(starts_ref, gates_ref, qkv_ref, local_ref, *refs):
    chunks, (out_ref, store_ref, sems) = refs[:-3], refs[-3:]
    copies, row = [], 0
    for i, chunk in enumerate(chunks):
        rows = chunk.shape[0]
        copies.append(
            pltpu.make_async_copy(chunk, store_ref.at[pl.ds(row, rows)], sems.at[i])
        )
        copies[-1].start()
        row += rows
    gates = [gates_ref[h : h + 1, :] for h in range(GROUPS)]
    query_blocks = qkv_ref.shape[0] // QBLOCK
    for copy in copies:
        copy.wait()

    for first in range(0, query_blocks, TOGETHER):
        indices = range(first, first + TOGETHER)
        places = [index * QBLOCK for index in indices]
        starts = [
            [pl.multiple_of(starts_ref[divmod(index * TOPB + j, TILE)], BLOCK) for j in range(TOPB)] for index in indices
        ]
        scores = []
        for lo, rows in zip(places, starts):
            query = heads_to_rows(qkv_ref[pl.ds(lo, QBLOCK), :LANES])
            scores.append(product(query, picked(store_ref, rows, slice(0, HEAD_DIM)), 1))
        tops = [jnp.max(score, axis=-1, keepdims=True) for score in scores]
        weights = [jnp.exp2((score - top) * EXP2_SCALE) for score, top in zip(scores, tops)]
        totals = [jnp.sum(weight, axis=-1, keepdims=True) for weight in weights]
        summed = [
            product(
                weight.astype(jnp.bfloat16),
                picked(store_ref, rows, slice(HEAD_DIM, 2 * HEAD_DIM)),
                0,
            )
            for weight, rows in zip(weights, starts)
        ]
        for lo, total, value in zip(places, totals, summed):
            for h in range(GROUPS):
                lanes = slice(h * HEAD_DIM, (h + 1) * HEAD_DIM)
                rows = slice(h * QBLOCK, (h + 1) * QBLOCK)
                memory_out = value[rows] * (gates[h] / total[rows])
                mixed = memory_out + (1.0 - gates[h]) * local_ref[pl.ds(lo, QBLOCK), lanes]
                out_ref[pl.ds(lo, QBLOCK), lanes] = mixed.astype(jnp.bfloat16)


BOTH = ("mem", "ctx")
SIDE = 8
CTX = 8


def device(z, y, ctx):
    return (z * SIDE + y) * CTX + ctx


def ring_of(ctx):
    return ctx % 2


def first_groups():
    groups = []
    for ctx in range(CTX):
        for other in range(SIDE):
            if ring_of(ctx) == 0:
                groups.append([device(z, other, ctx) for z in range(SIDE)])
            else:
                groups.append([device(other, y, ctx) for y in range(SIDE)])
    return groups


def moved(value, target):
    pairs = []
    for z in range(SIDE):
        for y in range(SIDE):
            for ctx in range(CTX):
                if ring_of(ctx) == 0:
                    to = device(z, target(y) % SIDE, ctx)
                else:
                    to = device(target(z) % SIDE, y, ctx)
                pairs.append((device(z, y, ctx), to))
    return lax.ppermute(value, BOTH, pairs)


def shifted(value, step):
    return moved(value, lambda place: place + step)


def ring_place():
    mem = lax.axis_index("mem")
    return jnp.where(lax.axis_index("ctx") % 2 == 0, mem % SIDE, mem // SIDE)


def gathered(chunk):
    ahead1, behind1 = shifted(chunk, 1), shifted(chunk, -1)
    ahead2, behind2 = shifted(ahead1, 1), shifted(behind1, -1)
    ahead3, behind3 = shifted(ahead2, 1), shifted(behind2, -1)
    onward = jnp.where(ring_place() % 2 == 0, ahead2, behind2)
    far = moved(onward, lambda place: place + 2 if place % 2 == 0 else place - 2)
    return [chunk, ahead1, ahead2, ahead3, far, behind3, behind2, behind1]


def body(queries, local_keys, local_values, mem_keys, mem_values, block_ids, gate_bias):
    tokens = queries.shape[0]
    members = lax.axis_size("ctx")
    span = tokens * members
    rows = mem_keys.shape[0]
    vmem = pl.BlockSpec(memory_space=pltpu.VMEM)
    smem = pl.BlockSpec(memory_space=pltpu.SMEM)
    hbm = pl.BlockSpec(memory_space=pl.ANY)
    packed, spread = pl.pallas_call(
        pack_kernel,
        out_shape=(
            jax.ShapeDtypeStruct((members, tokens, LANES + 3 * HEAD_DIM), jnp.bfloat16),
            jax.ShapeDtypeStruct((SIDE, rows, 2 * HEAD_DIM), jnp.bfloat16),
        ),
        in_specs=[smem] + [vmem] * 5,
        out_specs=(vmem, vmem),
        scratch_shapes=[pltpu.VMEM((tokens, HEAD_DIM), jnp.float32)],
        cost_estimate=pl.CostEstimate(flops=0, bytes_accessed=4 << 20, transcendentals=0),
    )(block_ids, queries, local_keys, local_values, mem_keys, mem_values)
    qkv = lax.all_to_all(packed, "ctx", split_axis=0, concat_axis=0, tiled=True)
    qkv = qkv.reshape(span, LANES + 3 * HEAD_DIM)
    chunk = lax.all_to_all(
        spread, BOTH, split_axis=0, concat_axis=0, tiled=True, axis_index_groups=first_groups()
    ).reshape(SIDE * rows, 2 * HEAD_DIM)
    chunks = gathered(chunk)
    local_out, starts, gates = pl.pallas_call(
        functools.partial(local_kernel, rows // BLOCK, rows),
        out_shape=(
            jax.ShapeDtypeStruct((span, LANES), jnp.float32),
            jax.ShapeDtypeStruct((span // TILE, TILE), jnp.int32),
            jax.ShapeDtypeStruct((GROUPS, HEAD_DIM), jnp.float32),
        ),
        in_specs=[smem, vmem],
        out_specs=(vmem, vmem, vmem),
        compiler_params=pltpu.CompilerParams(vmem_limit_bytes=12 << 20),
        cost_estimate=pl.CostEstimate(
            flops=4 * span * LANES * span, bytes_accessed=2 << 20, transcendentals=span * span * 4
        ),
    )(gate_bias, qkv)
    mixed = pl.pallas_call(
        memory_kernel,
        out_shape=jax.ShapeDtypeStruct((span, LANES), jnp.bfloat16),
        in_specs=[smem, vmem, vmem, vmem] + [hbm] * len(chunks),
        out_specs=vmem,
        scratch_shapes=[
            pltpu.VMEM((SIDE * SIDE * rows, 2 * HEAD_DIM), jnp.bfloat16),
            pltpu.SemaphoreType.DMA((len(chunks),)),
        ],
        compiler_params=pltpu.CompilerParams(vmem_limit_bytes=32 << 20),
        cost_estimate=pl.CostEstimate(
            flops=4 * span * LANES * TOPB * BLOCK,
            bytes_accessed=7 << 20,
            transcendentals=span * GROUPS * TOPB * BLOCK,
        ),
    )(starts, gates, qkv, local_out, *chunks)
    back = lax.all_to_all(
        mixed.reshape(members, tokens, LANES), "ctx", split_axis=0, concat_axis=0, tiled=True
    )
    return jnp.transpose(back, (1, 0, 2)).reshape(tokens, HEADS * HEAD_DIM)


def solution(mesh):
    return jax.shard_map(
        body,
        mesh=mesh,
        in_specs=(
            P(("mem", "ctx"), None),
            P(("mem", "ctx"), None),
            P(("mem", "ctx"), None),
            P("mem", None),
            P("mem", None),
            P(("mem", "ctx"), None),
            P(),
        ),
        out_specs=P(("mem", "ctx"), None),
        check_vma=False,
    )
```

```python
import functools

import jax
import jax.numpy as jnp
from jax import lax
from jax.experimental import pallas as pl
from jax.experimental.pallas import tpu as pltpu
from jax.sharding import PartitionSpec as P

HEADS = 32
KV_HEADS = 8
GROUPS = HEADS // KV_HEADS
HEAD_DIM = 128
BLOCK = 32
TOPB = 16
QBLOCK = 16
LANES = GROUPS * HEAD_DIM
EXP2_SCALE = HEAD_DIM ** (-0.5) * 1.4426950408889634
NEG = -1e30
TILE = 128
TOGETHER = 32


def product(left, right, contract_right):
    return lax.dot_general(
        left, right, (((1,), (contract_right,)), ((), ())), preferred_element_type=jnp.float32
    )


def softmax_parts(scores):
    top = jnp.max(scores, axis=-1, keepdims=True)
    weights = jnp.exp2((scores - top) * EXP2_SCALE)
    return weights, jnp.sum(weights, axis=-1, keepdims=True)


def heads_to_rows(rows):
    return jnp.concatenate(
        [rows[:, h * HEAD_DIM : (h + 1) * HEAD_DIM] for h in range(GROUPS)], axis=0
    )


def pack_kernel(ids_ref, queries_ref, keys_ref, values_ref, out_ref, id_ref):
    for block in range(ids_ref.shape[0]):
        for j in range(TOPB):
            value = ids_ref[block, j].astype(jnp.float32)
            id_ref[block * TOPB + j : block * TOPB + j + 1, :] = jnp.full(
                (1, HEAD_DIM), value, jnp.float32
            )
    id_lanes = id_ref[...].astype(jnp.bfloat16)
    for head in range(KV_HEADS):
        here = slice(head * HEAD_DIM, (head + 1) * HEAD_DIM)
        out_ref[head, :, :LANES] = queries_ref[:, head * LANES : (head + 1) * LANES]
        out_ref[head, :, LANES : LANES + HEAD_DIM] = keys_ref[:, here]
        out_ref[head, :, LANES + HEAD_DIM : LANES + 2 * HEAD_DIM] = values_ref[:, here]
        out_ref[head, :, LANES + 2 * HEAD_DIM :] = id_lanes


def block_rows(ids, held, rows):
    holder, slot = ids // held, ids % held
    z, y = holder // SIDE, holder % SIDE
    mem = lax.axis_index("mem")
    own_z, own_y = mem // SIDE, mem % SIDE
    first = lax.axis_index("ctx") % 2 == 0
    back = (jnp.where(first, own_y - y, own_z - z) + SIDE) % SIDE
    inner = jnp.where(first, z, y)
    return (back * SIDE + inner) * rows + slot * BLOCK


def local_kernel(held, rows, bias_ref, qkv_ref, out_ref, starts_ref, gates_ref):
    head = lax.axis_index("ctx")
    for h in range(GROUPS):
        bias = jnp.full((1, HEAD_DIM), bias_ref[head * GROUPS + h], jnp.float32)
        gates_ref[h : h + 1, :] = jax.nn.sigmoid(bias)
    span = qkv_ref.shape[0]
    diagonal = lax.broadcasted_iota(jnp.int32, (TILE, HEAD_DIM), 0) == lax.broadcasted_iota(
        jnp.int32, (TILE, HEAD_DIM), 1
    )
    for tile in range(span // TILE):
        ids = qkv_ref[tile * TILE : (tile + 1) * TILE, LANES + 2 * HEAD_DIM :].astype(jnp.float32)
        ids = jnp.sum(jnp.where(diagonal, ids, 0.0), axis=0, keepdims=True).astype(jnp.int32)
        starts_ref[tile : tile + 1, :] = block_rows(ids, held, rows)
    for tile in range(span // TILE):
        lo, hi = tile * TILE, (tile + 1) * TILE
        query = heads_to_rows(qkv_ref[lo:hi, :LANES])
        keys = qkv_ref[:hi, LANES : LANES + HEAD_DIM]
        values = qkv_ref[:hi, LANES + HEAD_DIM : LANES + 2 * HEAD_DIM]
        scores = product(query, keys, 1)
        row = lax.broadcasted_iota(jnp.int32, scores.shape, 0) % TILE + lo
        col = lax.broadcasted_iota(jnp.int32, scores.shape, 1)
        scores = jnp.where(col <= row, scores, NEG)
        weights, total = softmax_parts(scores)
        summed = product(weights.astype(jnp.bfloat16), values, 0) / total
        for h in range(GROUPS):
            out_ref[lo:hi, h * HEAD_DIM : (h + 1) * HEAD_DIM] = summed[
                h * TILE : (h + 1) * TILE
            ]


def picked(store_ref, rows, lanes):
    return jnp.concatenate([store_ref[pl.ds(row, BLOCK), lanes] for row in rows], axis=0)


def memory_kernel(starts_ref, gates_ref, qkv_ref, local_ref, *refs):
    chunks, (out_ref, store_ref, sems) = refs[:-3], refs[-3:]
    copies, row = [], 0
    for i, chunk in enumerate(chunks):
        rows = chunk.shape[0]
        copies.append(
            pltpu.make_async_copy(chunk, store_ref.at[pl.ds(row, rows)], sems.at[i])
        )
        copies[-1].start()
        row += rows
    gates = [gates_ref[h : h + 1, :] for h in range(GROUPS)]
    query_blocks = qkv_ref.shape[0] // QBLOCK
    for copy in copies:
        copy.wait()

    for first in range(0, query_blocks, TOGETHER):
        indices = range(first, first + TOGETHER)
        places = [index * QBLOCK for index in indices]
        starts = [
            [pl.multiple_of(starts_ref[divmod(index * TOPB + j, TILE)], BLOCK) for j in range(TOPB)] for index in indices
        ]
        scores = []
        for lo, rows in zip(places, starts):
            query = heads_to_rows(qkv_ref[pl.ds(lo, QBLOCK), :LANES])
            scores.append(product(query, picked(store_ref, rows, slice(0, HEAD_DIM)), 1))
        tops = [jnp.max(score, axis=-1, keepdims=True) for score in scores]
        weights = [jnp.exp2((score - top) * EXP2_SCALE) for score, top in zip(scores, tops)]
        totals = [jnp.sum(weight, axis=-1, keepdims=True) for weight in weights]
        summed = [
            product(
                weight.astype(jnp.bfloat16),
                picked(store_ref, rows, slice(HEAD_DIM, 2 * HEAD_DIM)),
                0,
            )
            for weight, rows in zip(weights, starts)
        ]
        for lo, total, value in zip(places, totals, summed):
            for h in range(GROUPS):
                lanes = slice(h * HEAD_DIM, (h + 1) * HEAD_DIM)
                rows = slice(h * QBLOCK, (h + 1) * QBLOCK)
                memory_out = value[rows] * (gates[h] / total[rows])
                mixed = memory_out + (1.0 - gates[h]) * local_ref[pl.ds(lo, QBLOCK), lanes]
                out_ref[pl.ds(lo, QBLOCK), lanes] = mixed.astype(jnp.bfloat16)


BOTH = ("mem", "ctx")
SIDE = 8
CTX = 8


def device(z, y, ctx):
    return (z * SIDE + y) * CTX + ctx


def ring_of(ctx):
    return ctx % 2


def first_groups():
    groups = []
    for ctx in range(CTX):
        for other in range(SIDE):
            if ring_of(ctx) == 0:
                groups.append([device(z, other, ctx) for z in range(SIDE)])
            else:
                groups.append([device(other, y, ctx) for y in range(SIDE)])
    return groups


def moved(value, target):
    pairs = []
    for z in range(SIDE):
        for y in range(SIDE):
            for ctx in range(CTX):
                if ring_of(ctx) == 0:
                    to = device(z, target(y) % SIDE, ctx)
                else:
                    to = device(target(z) % SIDE, y, ctx)
                pairs.append((device(z, y, ctx), to))
    return lax.ppermute(value, BOTH, pairs)


def shifted(value, step):
    return moved(value, lambda place: place + step)


def ring_place():
    mem = lax.axis_index("mem")
    return jnp.where(lax.axis_index("ctx") % 2 == 0, mem % SIDE, mem // SIDE)


def gathered(chunk):
    ahead2, behind2 = shifted(chunk, 2), shifted(chunk, -2)
    ahead1, behind1 = shifted(chunk, 1), shifted(chunk, -1)
    ahead3, behind3 = shifted(ahead2, 1), shifted(behind2, -1)
    onward = jnp.where(ring_place() % 2 == 0, ahead2, behind2)
    far = moved(onward, lambda place: place + 2 if place % 2 == 0 else place - 2)
    return [chunk, ahead1, ahead2, ahead3, far, behind3, behind2, behind1]


def body(queries, local_keys, local_values, mem_keys, mem_values, block_ids, gate_bias):
    tokens = queries.shape[0]
    members = lax.axis_size("ctx")
    span = tokens * members
    rows = mem_keys.shape[0]
    vmem = pl.BlockSpec(memory_space=pltpu.VMEM)
    smem = pl.BlockSpec(memory_space=pltpu.SMEM)
    hbm = pl.BlockSpec(memory_space=pl.ANY)
    start = lax.axis_index("ctx") * HEAD_DIM
    own = jnp.concatenate(
        [
            lax.dynamic_slice_in_dim(mem_keys, start, HEAD_DIM, 1),
            lax.dynamic_slice_in_dim(mem_values, start, HEAD_DIM, 1),
        ],
        axis=1,
    )
    spread = jnp.broadcast_to(own[None], (SIDE,) + own.shape)
    packed = pl.pallas_call(
        pack_kernel,
        out_shape=jax.ShapeDtypeStruct((members, tokens, LANES + 3 * HEAD_DIM), jnp.bfloat16),
        in_specs=[smem] + [vmem] * 3,
        out_specs=vmem,
        scratch_shapes=[pltpu.VMEM((tokens, HEAD_DIM), jnp.float32)],
        compiler_params=pltpu.CompilerParams(vmem_limit_bytes=8 << 20),
        cost_estimate=pl.CostEstimate(flops=0, bytes_accessed=2 << 20, transcendentals=0),
    )(block_ids, queries, local_keys, local_values)
    qkv = lax.all_to_all(packed, "ctx", split_axis=0, concat_axis=0, tiled=True)
    qkv = qkv.reshape(span, LANES + 3 * HEAD_DIM)
    chunk = lax.all_to_all(
        spread, BOTH, split_axis=0, concat_axis=0, tiled=True, axis_index_groups=first_groups()
    ).reshape(SIDE * rows, 2 * HEAD_DIM)
    chunks = gathered(chunk)
    local_out, starts, gates = pl.pallas_call(
        functools.partial(local_kernel, rows // BLOCK, rows),
        out_shape=(
            jax.ShapeDtypeStruct((span, LANES), jnp.float32),
            jax.ShapeDtypeStruct((span // TILE, TILE), jnp.int32),
            jax.ShapeDtypeStruct((GROUPS, HEAD_DIM), jnp.float32),
        ),
        in_specs=[smem, vmem],
        out_specs=(vmem, vmem, vmem),
        compiler_params=pltpu.CompilerParams(vmem_limit_bytes=12 << 20),
        cost_estimate=pl.CostEstimate(
            flops=4 * span * LANES * span, bytes_accessed=2 << 20, transcendentals=span * span * 4
        ),
    )(gate_bias, qkv)
    mixed = pl.pallas_call(
        memory_kernel,
        out_shape=jax.ShapeDtypeStruct((span, LANES), jnp.bfloat16),
        in_specs=[smem, vmem, vmem, vmem] + [hbm] * len(chunks),
        out_specs=vmem,
        scratch_shapes=[
            pltpu.VMEM((SIDE * SIDE * rows, 2 * HEAD_DIM), jnp.bfloat16),
            pltpu.SemaphoreType.DMA((len(chunks),)),
        ],
        compiler_params=pltpu.CompilerParams(vmem_limit_bytes=32 << 20),
        cost_estimate=pl.CostEstimate(
            flops=4 * span * LANES * TOPB * BLOCK,
            bytes_accessed=7 << 20,
            transcendentals=span * GROUPS * TOPB * BLOCK,
        ),
    )(starts, gates, qkv, local_out, *chunks)
    back = lax.all_to_all(
        mixed.reshape(members, tokens, LANES), "ctx", split_axis=0, concat_axis=0, tiled=True
    )
    return jnp.transpose(back, (1, 0, 2)).reshape(tokens, HEADS * HEAD_DIM)


def solution(mesh):
    return jax.shard_map(
        body,
        mesh=mesh,
        in_specs=(
            P(("mem", "ctx"), None),
            P(("mem", "ctx"), None),
            P(("mem", "ctx"), None),
            P("mem", None),
            P("mem", None),
            P(("mem", "ctx"), None),
            P(),
        ),
        out_specs=P(("mem", "ctx"), None),
        check_vma=False,
    )
```

```python
import functools

import jax
import jax.numpy as jnp
from jax import lax
from jax.experimental import pallas as pl
from jax.experimental.pallas import tpu as pltpu
from jax.sharding import PartitionSpec as P

HEADS = 32
KV_HEADS = 8
GROUPS = HEADS // KV_HEADS
HEAD_DIM = 128
BLOCK = 32
TOPB = 16
QBLOCK = 16
LANES = GROUPS * HEAD_DIM
EXP2_SCALE = HEAD_DIM ** (-0.5) * 1.4426950408889634
NEG = -1e30
TILE = 128
TOGETHER = 32


def product(left, right, contract_right):
    return lax.dot_general(
        left, right, (((1,), (contract_right,)), ((), ())), preferred_element_type=jnp.float32
    )


def softmax_parts(scores):
    top = jnp.max(scores, axis=-1, keepdims=True)
    weights = jnp.exp2((scores - top) * EXP2_SCALE)
    return weights, jnp.sum(weights, axis=-1, keepdims=True)


def heads_to_rows(rows):
    return jnp.concatenate(
        [rows[:, h * HEAD_DIM : (h + 1) * HEAD_DIM] for h in range(GROUPS)], axis=0
    )


def pack_kernel(ids_ref, queries_ref, keys_ref, values_ref, out_ref, id_ref):
    for block in range(ids_ref.shape[0]):
        for j in range(TOPB):
            value = ids_ref[block, j].astype(jnp.float32)
            id_ref[block * TOPB + j : block * TOPB + j + 1, :] = jnp.full(
                (1, HEAD_DIM), value, jnp.float32
            )
    id_lanes = id_ref[...].astype(jnp.bfloat16)
    for head in range(KV_HEADS):
        here = slice(head * HEAD_DIM, (head + 1) * HEAD_DIM)
        out_ref[head, :, :LANES] = queries_ref[:, head * LANES : (head + 1) * LANES]
        out_ref[head, :, LANES : LANES + HEAD_DIM] = keys_ref[:, here]
        out_ref[head, :, LANES + HEAD_DIM : LANES + 2 * HEAD_DIM] = values_ref[:, here]
        out_ref[head, :, LANES + 2 * HEAD_DIM :] = id_lanes


def block_rows(ids, held, rows):
    holder, slot = ids // held, ids % held
    z, y = holder // SIDE, holder % SIDE
    mem = lax.axis_index("mem")
    own_z, own_y = mem // SIDE, mem % SIDE
    first = lax.axis_index("ctx") % 2 == 0
    back = (jnp.where(first, own_y - y, own_z - z) + SIDE) % SIDE
    inner = jnp.where(first, z, y)
    return (back * SIDE + inner) * rows + slot * BLOCK


def local_kernel(held, rows, bias_ref, qkv_ref, out_ref, starts_ref, gates_ref):
    head = lax.axis_index("ctx")
    for h in range(GROUPS):
        bias = jnp.full((1, HEAD_DIM), bias_ref[head * GROUPS + h], jnp.float32)
        gates_ref[h : h + 1, :] = jax.nn.sigmoid(bias)
    span = qkv_ref.shape[0]
    diagonal = lax.broadcasted_iota(jnp.int32, (TILE, HEAD_DIM), 0) == lax.broadcasted_iota(
        jnp.int32, (TILE, HEAD_DIM), 1
    )
    for tile in range(span // TILE):
        ids = qkv_ref[tile * TILE : (tile + 1) * TILE, LANES + 2 * HEAD_DIM :].astype(jnp.float32)
        ids = jnp.sum(jnp.where(diagonal, ids, 0.0), axis=0, keepdims=True).astype(jnp.int32)
        starts_ref[tile : tile + 1, :] = block_rows(ids, held, rows)
    for tile in range(span // TILE):
        lo, hi = tile * TILE, (tile + 1) * TILE
        query = heads_to_rows(qkv_ref[lo:hi, :LANES])
        keys = qkv_ref[:hi, LANES : LANES + HEAD_DIM]
        values = qkv_ref[:hi, LANES + HEAD_DIM : LANES + 2 * HEAD_DIM]
        scores = product(query, keys, 1)
        row = lax.broadcasted_iota(jnp.int32, scores.shape, 0) % TILE + lo
        col = lax.broadcasted_iota(jnp.int32, scores.shape, 1)
        scores = jnp.where(col <= row, scores, NEG)
        weights, total = softmax_parts(scores)
        summed = product(weights.astype(jnp.bfloat16), values, 0) / total
        for h in range(GROUPS):
            out_ref[lo:hi, h * HEAD_DIM : (h + 1) * HEAD_DIM] = summed[
                h * TILE : (h + 1) * TILE
            ]


def picked(store_ref, rows, lanes):
    return jnp.concatenate([store_ref[pl.ds(row, BLOCK), lanes] for row in rows], axis=0)


def memory_kernel(starts_ref, gates_ref, qkv_ref, local_ref, *refs):
    chunks, (out_ref, store_ref, sems) = refs[:-3], refs[-3:]
    copies, row = [], 0
    for i, chunk in enumerate(chunks):
        rows = chunk.shape[0]
        copies.append(
            pltpu.make_async_copy(chunk, store_ref.at[pl.ds(row, rows)], sems.at[i])
        )
        copies[-1].start()
        row += rows
    gates = [gates_ref[h : h + 1, :] for h in range(GROUPS)]
    query_blocks = qkv_ref.shape[0] // QBLOCK
    for copy in copies:
        copy.wait()

    for first in range(0, query_blocks, TOGETHER):
        indices = range(first, first + TOGETHER)
        places = [index * QBLOCK for index in indices]
        starts = [
            [pl.multiple_of(starts_ref[divmod(index * TOPB + j, TILE)], BLOCK) for j in range(TOPB)] for index in indices
        ]
        scores = []
        for lo, rows in zip(places, starts):
            query = heads_to_rows(qkv_ref[pl.ds(lo, QBLOCK), :LANES])
            scores.append(product(query, picked(store_ref, rows, slice(0, HEAD_DIM)), 1))
        tops = [jnp.max(score, axis=-1, keepdims=True) for score in scores]
        weights = [jnp.exp2((score - top) * EXP2_SCALE) for score, top in zip(scores, tops)]
        totals = [jnp.sum(weight, axis=-1, keepdims=True) for weight in weights]
        summed = [
            product(
                weight.astype(jnp.bfloat16),
                picked(store_ref, rows, slice(HEAD_DIM, 2 * HEAD_DIM)),
                0,
            )
            for weight, rows in zip(weights, starts)
        ]
        for lo, total, value in zip(places, totals, summed):
            for h in range(GROUPS):
                lanes = slice(h * HEAD_DIM, (h + 1) * HEAD_DIM)
                rows = slice(h * QBLOCK, (h + 1) * QBLOCK)
                memory_out = value[rows] * (gates[h] / total[rows])
                mixed = memory_out + (1.0 - gates[h]) * local_ref[pl.ds(lo, QBLOCK), lanes]
                out_ref[pl.ds(lo, QBLOCK), lanes] = mixed.astype(jnp.bfloat16)


BOTH = ("mem", "ctx")
SIDE = 8
CTX = 8


def device(z, y, ctx):
    return (z * SIDE + y) * CTX + ctx


def ring_of(ctx):
    return ctx % 2


def first_groups():
    groups = []
    for ctx in range(CTX):
        for other in range(SIDE):
            if ring_of(ctx) == 0:
                groups.append([device(z, other, ctx) for z in range(SIDE)])
            else:
                groups.append([device(other, y, ctx) for y in range(SIDE)])
    return groups


def moved(value, target):
    pairs = []
    for z in range(SIDE):
        for y in range(SIDE):
            for ctx in range(CTX):
                if ring_of(ctx) == 0:
                    to = device(z, target(y) % SIDE, ctx)
                else:
                    to = device(target(z) % SIDE, y, ctx)
                pairs.append((device(z, y, ctx), to))
    return lax.ppermute(value, BOTH, pairs)


def shifted(value, step):
    return moved(value, lambda place: place + step)


def ring_place():
    mem = lax.axis_index("mem")
    return jnp.where(lax.axis_index("ctx") % 2 == 0, mem % SIDE, mem // SIDE)


def gathered(chunk):
    ahead2, behind2 = shifted(chunk, 2), shifted(chunk, -2)
    ahead1, behind1 = shifted(chunk, 1), shifted(chunk, -1)
    ahead3, behind3 = shifted(ahead2, 1), shifted(behind2, -1)
    onward = jnp.where(ring_place() % 2 == 0, ahead2, behind2)
    far = moved(onward, lambda place: place + 2 if place % 2 == 0 else place - 2)
    return [chunk, ahead1, ahead2, ahead3, far, behind3, behind2, behind1]


def body(queries, local_keys, local_values, mem_keys, mem_values, block_ids, gate_bias):
    tokens = queries.shape[0]
    members = lax.axis_size("ctx")
    span = tokens * members
    rows = mem_keys.shape[0]
    vmem = pl.BlockSpec(memory_space=pltpu.VMEM)
    smem = pl.BlockSpec(memory_space=pltpu.SMEM)
    hbm = pl.BlockSpec(memory_space=pl.ANY)
    start = lax.axis_index("ctx") * HEAD_DIM
    own = jnp.concatenate(
        [
            lax.dynamic_slice_in_dim(mem_keys, start, HEAD_DIM, 1),
            lax.dynamic_slice_in_dim(mem_values, start, HEAD_DIM, 1),
        ],
        axis=1,
    )
    spread = jnp.broadcast_to(own[None], (SIDE,) + own.shape)
    packed = pl.pallas_call(
        pack_kernel,
        out_shape=jax.ShapeDtypeStruct((members, tokens, LANES + 3 * HEAD_DIM), jnp.bfloat16),
        in_specs=[smem] + [vmem] * 3,
        out_specs=vmem,
        scratch_shapes=[pltpu.VMEM((tokens, HEAD_DIM), jnp.float32)],
        compiler_params=pltpu.CompilerParams(vmem_limit_bytes=8 << 20),
        cost_estimate=pl.CostEstimate(flops=0, bytes_accessed=2 << 20, transcendentals=0),
    )(block_ids, queries, local_keys, local_values)
    chunk = lax.all_to_all(
        spread, BOTH, split_axis=0, concat_axis=0, tiled=True, axis_index_groups=first_groups()
    ).reshape(SIDE * rows, 2 * HEAD_DIM)
    packed, chunk = lax.optimization_barrier((packed, chunk))
    qkv = lax.all_to_all(packed, "ctx", split_axis=0, concat_axis=0, tiled=True)
    qkv = qkv.reshape(span, LANES + 3 * HEAD_DIM)
    chunks = gathered(chunk)
    local_out, starts, gates = pl.pallas_call(
        functools.partial(local_kernel, rows // BLOCK, rows),
        out_shape=(
            jax.ShapeDtypeStruct((span, LANES), jnp.float32),
            jax.ShapeDtypeStruct((span // TILE, TILE), jnp.int32),
            jax.ShapeDtypeStruct((GROUPS, HEAD_DIM), jnp.float32),
        ),
        in_specs=[smem, vmem],
        out_specs=(vmem, vmem, vmem),
        compiler_params=pltpu.CompilerParams(vmem_limit_bytes=12 << 20),
        cost_estimate=pl.CostEstimate(
            flops=4 * span * LANES * span, bytes_accessed=2 << 20, transcendentals=span * span * 4
        ),
    )(gate_bias, qkv)
    mixed = pl.pallas_call(
        memory_kernel,
        out_shape=jax.ShapeDtypeStruct((span, LANES), jnp.bfloat16),
        in_specs=[smem, vmem, vmem, vmem] + [hbm] * len(chunks),
        out_specs=vmem,
        scratch_shapes=[
            pltpu.VMEM((SIDE * SIDE * rows, 2 * HEAD_DIM), jnp.bfloat16),
            pltpu.SemaphoreType.DMA((len(chunks),)),
        ],
        compiler_params=pltpu.CompilerParams(vmem_limit_bytes=32 << 20),
        cost_estimate=pl.CostEstimate(
            flops=4 * span * LANES * TOPB * BLOCK,
            bytes_accessed=7 << 20,
            transcendentals=span * GROUPS * TOPB * BLOCK,
        ),
    )(starts, gates, qkv, local_out, *chunks)
    back = lax.all_to_all(
        mixed.reshape(members, tokens, LANES), "ctx", split_axis=0, concat_axis=0, tiled=True
    )
    return jnp.transpose(back, (1, 0, 2)).reshape(tokens, HEADS * HEAD_DIM)


def solution(mesh):
    return jax.shard_map(
        body,
        mesh=mesh,
        in_specs=(
            P(("mem", "ctx"), None),
            P(("mem", "ctx"), None),
            P(("mem", "ctx"), None),
            P("mem", None),
            P("mem", None),
            P(("mem", "ctx"), None),
            P(),
        ),
        out_specs=P(("mem", "ctx"), None),
        check_vma=False,
    )
```

```python
import functools

import jax
import jax.numpy as jnp
from jax import lax
from jax.experimental import pallas as pl
from jax.experimental.pallas import tpu as pltpu
from jax.sharding import PartitionSpec as P

HEADS = 32
KV_HEADS = 8
GROUPS = HEADS // KV_HEADS
HEAD_DIM = 128
BLOCK = 32
TOPB = 16
QBLOCK = 16
LANES = GROUPS * HEAD_DIM
EXP2_SCALE = HEAD_DIM ** (-0.5) * 1.4426950408889634
NEG = -1e30
TILE = 128
TOGETHER = 32


def product(left, right, contract_right):
    return lax.dot_general(
        left, right, (((1,), (contract_right,)), ((), ())), preferred_element_type=jnp.float32
    )


def softmax_parts(scores):
    top = jnp.max(scores, axis=-1, keepdims=True)
    weights = jnp.exp2((scores - top) * EXP2_SCALE)
    return weights, jnp.sum(weights, axis=-1, keepdims=True)


def heads_to_rows(rows):
    return jnp.concatenate(
        [rows[:, h * HEAD_DIM : (h + 1) * HEAD_DIM] for h in range(GROUPS)], axis=0
    )


def pack_kernel(ids_ref, queries_ref, keys_ref, values_ref, out_ref, id_ref):
    for block in range(ids_ref.shape[0]):
        for j in range(TOPB):
            value = ids_ref[block, j].astype(jnp.float32)
            id_ref[block * TOPB + j : block * TOPB + j + 1, :] = jnp.full(
                (1, HEAD_DIM), value, jnp.float32
            )
    id_lanes = id_ref[...].astype(jnp.bfloat16)
    for head in range(KV_HEADS):
        here = slice(head * HEAD_DIM, (head + 1) * HEAD_DIM)
        out_ref[head, :, :LANES] = queries_ref[:, head * LANES : (head + 1) * LANES]
        out_ref[head, :, LANES : LANES + HEAD_DIM] = keys_ref[:, here]
        out_ref[head, :, LANES + HEAD_DIM : LANES + 2 * HEAD_DIM] = values_ref[:, here]
        out_ref[head, :, LANES + 2 * HEAD_DIM :] = id_lanes


def block_rows(ids, held, rows):
    holder, slot = ids // held, ids % held
    z, y = holder // SIDE, holder % SIDE
    mem = lax.axis_index("mem")
    own_z, own_y = mem // SIDE, mem % SIDE
    first = lax.axis_index("ctx") % 2 == 0
    back = (jnp.where(first, own_y - y, own_z - z) + SIDE) % SIDE
    inner = jnp.where(first, z, y)
    return (back * SIDE + inner) * rows + slot * BLOCK


def local_kernel(held, rows, bias_ref, qkv_ref, out_ref, starts_ref, gates_ref):
    head = lax.axis_index("ctx")
    for h in range(GROUPS):
        bias = jnp.full((1, HEAD_DIM), bias_ref[head * GROUPS + h], jnp.float32)
        gates_ref[h : h + 1, :] = jax.nn.sigmoid(bias)
    span = qkv_ref.shape[0]
    diagonal = lax.broadcasted_iota(jnp.int32, (TILE, HEAD_DIM), 0) == lax.broadcasted_iota(
        jnp.int32, (TILE, HEAD_DIM), 1
    )
    for tile in range(span // TILE):
        ids = qkv_ref[tile * TILE : (tile + 1) * TILE, LANES + 2 * HEAD_DIM :].astype(jnp.float32)
        ids = jnp.sum(jnp.where(diagonal, ids, 0.0), axis=0, keepdims=True).astype(jnp.int32)
        starts_ref[tile : tile + 1, :] = block_rows(ids, held, rows)
    for tile in range(span // TILE):
        lo, hi = tile * TILE, (tile + 1) * TILE
        query = heads_to_rows(qkv_ref[lo:hi, :LANES])
        keys = qkv_ref[:hi, LANES : LANES + HEAD_DIM]
        values = qkv_ref[:hi, LANES + HEAD_DIM : LANES + 2 * HEAD_DIM]
        scores = product(query, keys, 1)
        row = lax.broadcasted_iota(jnp.int32, scores.shape, 0) % TILE + lo
        col = lax.broadcasted_iota(jnp.int32, scores.shape, 1)
        scores = jnp.where(col <= row, scores, NEG)
        weights, total = softmax_parts(scores)
        summed = product(weights.astype(jnp.bfloat16), values, 0) / total
        for h in range(GROUPS):
            out_ref[lo:hi, h * HEAD_DIM : (h + 1) * HEAD_DIM] = summed[
                h * TILE : (h + 1) * TILE
            ]


def picked(store_ref, rows, lanes):
    return jnp.concatenate([store_ref[pl.ds(row, BLOCK), lanes] for row in rows], axis=0)


def memory_kernel(starts_ref, gates_ref, qkv_ref, local_ref, *refs):
    chunks, (out_ref, store_ref, sems) = refs[:-3], refs[-3:]
    copies, row = [], 0
    for i, chunk in enumerate(chunks):
        rows = chunk.shape[0]
        copies.append(
            pltpu.make_async_copy(chunk, store_ref.at[pl.ds(row, rows)], sems.at[i])
        )
        copies[-1].start()
        row += rows
    gates = [gates_ref[h : h + 1, :] for h in range(GROUPS)]
    query_blocks = qkv_ref.shape[0] // QBLOCK
    for copy in copies:
        copy.wait()

    for first in range(0, query_blocks, TOGETHER):
        indices = range(first, first + TOGETHER)
        places = [index * QBLOCK for index in indices]
        starts = [
            [pl.multiple_of(starts_ref[divmod(index * TOPB + j, TILE)], BLOCK) for j in range(TOPB)] for index in indices
        ]
        scores = []
        for lo, rows in zip(places, starts):
            query = heads_to_rows(qkv_ref[pl.ds(lo, QBLOCK), :LANES])
            scores.append(product(query, picked(store_ref, rows, slice(0, HEAD_DIM)), 1))
        tops = [jnp.max(score, axis=-1, keepdims=True) for score in scores]
        weights = [jnp.exp2((score - top) * EXP2_SCALE) for score, top in zip(scores, tops)]
        totals = [jnp.sum(weight, axis=-1, keepdims=True) for weight in weights]
        summed = [
            product(
                weight.astype(jnp.bfloat16),
                picked(store_ref, rows, slice(HEAD_DIM, 2 * HEAD_DIM)),
                0,
            )
            for weight, rows in zip(weights, starts)
        ]
        for lo, total, value in zip(places, totals, summed):
            for h in range(GROUPS):
                lanes = slice(h * HEAD_DIM, (h + 1) * HEAD_DIM)
                rows = slice(h * QBLOCK, (h + 1) * QBLOCK)
                memory_out = value[rows] * (gates[h] / total[rows])
                mixed = memory_out + (1.0 - gates[h]) * local_ref[pl.ds(lo, QBLOCK), lanes]
                out_ref[pl.ds(lo, QBLOCK), lanes] = mixed.astype(jnp.bfloat16)


BOTH = ("mem", "ctx")
SIDE = 8
CTX = 8


def device(z, y, ctx):
    return (z * SIDE + y) * CTX + ctx


def ring_of(ctx):
    return ctx % 2


def first_groups():
    groups = []
    for ctx in range(CTX):
        for other in range(SIDE):
            if ring_of(ctx) == 0:
                groups.append([device(z, other, ctx) for z in range(SIDE)])
            else:
                groups.append([device(other, y, ctx) for y in range(SIDE)])
    return groups


def moved(value, target):
    pairs = []
    for z in range(SIDE):
        for y in range(SIDE):
            for ctx in range(CTX):
                if ring_of(ctx) == 0:
                    to = device(z, target(y) % SIDE, ctx)
                else:
                    to = device(target(z) % SIDE, y, ctx)
                pairs.append((device(z, y, ctx), to))
    return lax.ppermute(value, BOTH, pairs)


def shifted(value, step):
    return moved(value, lambda place: place + step)


def ring_place():
    mem = lax.axis_index("mem")
    return jnp.where(lax.axis_index("ctx") % 2 == 0, mem % SIDE, mem // SIDE)


def gathered(chunk):
    ahead2, behind2 = shifted(chunk, 2), shifted(chunk, -2)
    ahead1, behind1 = shifted(chunk, 1), shifted(chunk, -1)
    ahead3, behind3 = shifted(ahead2, 1), shifted(behind2, -1)
    onward = jnp.where(ring_place() % 2 == 0, ahead2, behind2)
    far = moved(onward, lambda place: place + 2 if place % 2 == 0 else place - 2)
    return [chunk, ahead1, ahead2, ahead3, far, behind3, behind2, behind1]


def body(queries, local_keys, local_values, mem_keys, mem_values, block_ids, gate_bias):
    tokens = queries.shape[0]
    members = lax.axis_size("ctx")
    span = tokens * members
    rows = mem_keys.shape[0]
    vmem = pl.BlockSpec(memory_space=pltpu.VMEM)
    smem = pl.BlockSpec(memory_space=pltpu.SMEM)
    hbm = pl.BlockSpec(memory_space=pl.ANY)
    start = lax.axis_index("ctx") * HEAD_DIM
    own = jnp.concatenate(
        [
            lax.dynamic_slice_in_dim(mem_keys, start, HEAD_DIM, 1),
            lax.dynamic_slice_in_dim(mem_values, start, HEAD_DIM, 1),
        ],
        axis=1,
    )
    spread = jnp.broadcast_to(own[None], (SIDE,) + own.shape)
    packed = pl.pallas_call(
        pack_kernel,
        out_shape=jax.ShapeDtypeStruct((members, tokens, LANES + 3 * HEAD_DIM), jnp.bfloat16),
        in_specs=[smem] + [vmem] * 3,
        out_specs=vmem,
        scratch_shapes=[pltpu.VMEM((tokens, HEAD_DIM), jnp.float32)],
        compiler_params=pltpu.CompilerParams(vmem_limit_bytes=8 << 20),
        cost_estimate=pl.CostEstimate(flops=0, bytes_accessed=2 << 20, transcendentals=0),
    )(block_ids, queries, local_keys, local_values)
    qkv = lax.all_to_all(packed, "ctx", split_axis=0, concat_axis=0, tiled=True)
    qkv = qkv.reshape(span, LANES + 3 * HEAD_DIM)
    chunk = lax.all_to_all(
        spread, BOTH, split_axis=0, concat_axis=0, tiled=True, axis_index_groups=first_groups()
    ).reshape(SIDE * rows, 2 * HEAD_DIM)
    chunks = gathered(chunk)
    local_out, starts, gates = pl.pallas_call(
        functools.partial(local_kernel, rows // BLOCK, rows),
        out_shape=(
            jax.ShapeDtypeStruct((span, LANES), jnp.float32),
            jax.ShapeDtypeStruct((span // TILE, TILE), jnp.int32),
            jax.ShapeDtypeStruct((GROUPS, HEAD_DIM), jnp.float32),
        ),
        in_specs=[smem, vmem],
        out_specs=(vmem, vmem, vmem),
        compiler_params=pltpu.CompilerParams(vmem_limit_bytes=12 << 20),
        cost_estimate=pl.CostEstimate(
            flops=64 * span * LANES * span, bytes_accessed=2 << 20, transcendentals=span * span * 4
        ),
    )(gate_bias, qkv)
    mixed = pl.pallas_call(
        memory_kernel,
        out_shape=jax.ShapeDtypeStruct((span, LANES), jnp.bfloat16),
        in_specs=[smem, vmem, vmem, vmem] + [hbm] * len(chunks),
        out_specs=vmem,
        scratch_shapes=[
            pltpu.VMEM((SIDE * SIDE * rows, 2 * HEAD_DIM), jnp.bfloat16),
            pltpu.SemaphoreType.DMA((len(chunks),)),
        ],
        compiler_params=pltpu.CompilerParams(vmem_limit_bytes=32 << 20),
        cost_estimate=pl.CostEstimate(
            flops=4 * span * LANES * TOPB * BLOCK,
            bytes_accessed=7 << 20,
            transcendentals=span * GROUPS * TOPB * BLOCK,
        ),
    )(starts, gates, qkv, local_out, *chunks)
    back = lax.all_to_all(
        mixed.reshape(members, tokens, LANES), "ctx", split_axis=0, concat_axis=0, tiled=True
    )
    return jnp.transpose(back, (1, 0, 2)).reshape(tokens, HEADS * HEAD_DIM)


def solution(mesh):
    return jax.shard_map(
        body,
        mesh=mesh,
        in_specs=(
            P(("mem", "ctx"), None),
            P(("mem", "ctx"), None),
            P(("mem", "ctx"), None),
            P("mem", None),
            P("mem", None),
            P(("mem", "ctx"), None),
            P(),
        ),
        out_specs=P(("mem", "ctx"), None),
        check_vma=False,
    )
```
